512 devices in a mesh: wide: 32 (over x_lo, z), grp: 16 (over y, x_hi, core).
Axes of the slice: x: 4 (x_hi: 2, x_lo: 2; x = x_hi * 2 + x_lo), y: 4, z: 16, core: 2. Of those that a mesh axis runs over, the one named last changes fastest.
Arguments:
- log_hazards: float32 [25, 25], replicated, may hold values from -0.5 to 0.5
- bit_order: int32 [25], replicated, may hold values from 0 to 24, each once
- patients: int32 [256], replicated, may hold values from 0 to 33554431, as said below
- start_dist: float32 [33554432], P(('wide', 'grp')), may hold values from 0.25 to 4
- start_adjoint: float32 [33554432], P(('wide', 'grp')), may hold values from -6 to 6
Outputs:
- distribution: float32 [33554432], P(('wide', 'grp'))
- loglik: float32 [], replicated
- gradient: float32 [25, 25], replicated
- empty_state: float32 [], replicated
The draws below stay inside these ranges and needn't reach their ends.
Inputs may be any that keep to these rules, and one draw needn't show every extreme that they name: `patients`: each value is a set of events, bit e set when event e is present; every draw has a patient with no event and one with all 25. `bit_order`: A permutation of the events.
All inputs are finite; a program needn't handle non-finite values.
Results may differ from the reference program's by a relative error of at most 0.0003.
Values sent between devices are 32-bit elements; how exact they have to be, the bound alone decides.
A program may use at most 64 MiB of HBM per device.

```python
import math
import jax
import jax.numpy as jnp
from jax import lax

EVENTS = 25
PATIENTS = 256
FWD = 1
ADJ = 1
STATES = 33554432


def draw_patients(key, part):
    chance_key, throw_key, pick_key = jax.random.split(jax.random.fold_in(key, 7), 3)
    chances = jax.random.randint(chance_key, (EVENTS,), 1, 9)
    throws = jax.random.randint(throw_key, (PATIENTS, EVENTS), 0, 16)
    present = (throws < chances[None, :]).astype(jnp.int32)
    chosen = jax.random.randint(pick_key, (), 0, PATIENTS // 2)
    rows_seen = jnp.arange(PATIENTS, dtype=jnp.int32)
    present = jnp.where((rows_seen == chosen)[:, None], 1, present)
    present = jnp.where((rows_seen == chosen + PATIENTS // 2)[:, None], 0, present)
    shifts = jnp.arange(EVENTS, dtype=jnp.int32)
    return jnp.sum(present << shifts[None, :], axis=1).astype(jnp.int32)


def draw_start_adjoint(key, part):
    value_key = jax.random.fold_in(jax.random.fold_in(key, 11), 0)
    return jax.random.truncated_normal(value_key, -6.0, 6.0, (STATES,), jnp.float32).astype(jnp.float32)


def shard_levels(key, dims, pieces, smallest, high):
    gain = 1.0
    for position, blocks in pieces:
        draws = jax.random.uniform(jax.random.fold_in(jax.random.fold_in(key, 6), position), (blocks,), jnp.float32, smallest / len(pieces), high / len(pieces))
        gain = gain * jnp.repeat(jnp.exp(draws), dims[position] // blocks).reshape((-1,) + (1,) * (len(dims) - 1 - position))
    return gain


def setup_inputs(seed: int = 0) -> dict:
    splits = jax.random.split(jax.random.key(seed), 6)
    log_hazards = jnp.clip(jax.random.uniform(splits[0], (EVENTS, EVENTS), jnp.float32, -0.5, 0.5), -0.5, 0.5)
    bit_order = jax.random.permutation(splits[1], EVENTS).astype(jnp.int32)
    patients = draw_patients(jax.random.fold_in(splits[5], 71), 0)
    start_dist = jnp.clip(jnp.exp(math.log(4.0) - 2.7725887 * jax.random.uniform(splits[3], (STATES,), jnp.float32) ** shard_levels(splits[3], (STATES,), ((0, 512),), -0.2, 0.2)), 0.25, 4.0)
    start_adjoint = draw_start_adjoint(jax.random.fold_in(splits[5], 71), 0)
    return dict(log_hazards=log_hazards, bit_order=bit_order, patients=patients, start_dist=start_dist, start_adjoint=start_adjoint)


highest = lax.Precision.HIGHEST


def bit_table(number, columns):
    positions = jnp.arange(number, dtype=jnp.int32)
    shifts = jnp.arange(columns, dtype=jnp.int32)
    return ((positions[:, None] >> shifts[None, :]) & 1).astype(jnp.float32)


def halves(values, event_bit):
    return values.reshape(-1, 2, 2 ** event_bit)


def lower_only(values, event_bit):
    paired = halves(values, event_bit)
    return jnp.concatenate([paired[:, :1], jnp.zeros_like(paired[:, 1:])], axis=1).reshape(-1)


def push_up(values, event_bit):
    paired = halves(values, event_bit)
    return jnp.concatenate([jnp.zeros_like(paired[:, :1]), paired[:, :1]], axis=1).reshape(-1)


def pull_down(values, event_bit):
    paired = halves(values, event_bit)
    return jnp.concatenate([paired[:, 1:], jnp.zeros_like(paired[:, :1])], axis=1).reshape(-1)


def reference(log_hazards, bit_order, patients, start_dist, start_adjoint):
    count_bits = EVENTS
    low_bits = count_bits // 2
    high_bits = count_bits - low_bits
    states = 2 ** count_bits
    shifts = jnp.arange(count_bits, dtype=jnp.int32)
    onehot = (bit_order[:, None] == shifts[None, :]).astype(jnp.float32)
    by_bits = jnp.dot(onehot.T, jnp.dot(log_hazards, onehot, precision=highest), precision=highest)
    diagonal = jnp.diagonal(by_bits)
    coupling = by_bits * (1.0 - jnp.eye(count_bits, dtype=jnp.float32))
    low_table = bit_table(2 ** low_bits, low_bits)
    high_table = bit_table(2 ** high_bits, high_bits)
    low_part = jnp.dot(low_table, coupling[:, :low_bits].T, precision=highest)
    high_part = jnp.dot(high_table, coupling[:, low_bits:].T, precision=highest)

    def event_rate(event_bit):
        return jnp.exp(diagonal[event_bit] + high_part[:, event_bit][:, None] + low_part[:, event_bit][None, :]).reshape(-1)

    denominator = jnp.ones((states,), jnp.float32)
    for event_bit in range(count_bits):
        denominator = denominator + lower_only(event_rate(event_bit), event_bit)
    source = jnp.zeros((states,), jnp.float32).at[0].set(float(states))
    forward = start_dist
    for repeat in range(FWD):
        summed = source
        for event_bit in range(count_bits):
            summed = summed + push_up(event_rate(event_bit) * forward, event_bit)
        forward = summed / denominator
    present = (patients[:, None] >> shifts[None, :]) & 1
    state_index = jnp.sum(present << bit_order[None, :], axis=1).astype(jnp.int32)
    counts = jnp.zeros((states,), jnp.float32).at[state_index].add(1.0)
    loglik = jnp.sum(jnp.log(forward[state_index])) / PATIENTS
    weights = counts / (PATIENTS * forward)
    adjoint = start_adjoint * (2.0 ** (-(count_bits // 2)))
    for repeat in range(ADJ):
        summed = weights
        for event_bit in range(count_bits):
            summed = summed + event_rate(event_bit) * pull_down(adjoint, event_bit)
        adjoint = summed / denominator
    grad_rows = []
    for event_bit in range(count_bits):
        contrib = lower_only(event_rate(event_bit) * forward * (pull_down(adjoint, event_bit) - adjoint), event_bit)
        square = contrib.reshape(2 ** high_bits, 2 ** low_bits)
        low_sum = jnp.dot(jnp.sum(square, axis=0), low_table, precision=highest)
        high_sum = jnp.dot(jnp.sum(square, axis=1), high_table, precision=highest)
        own_column = (shifts == event_bit).astype(jnp.float32)
        grad_rows.append(jnp.concatenate([low_sum, high_sum]) + jnp.sum(contrib) * own_column)
    by_bit_grad = jnp.stack(grad_rows)
    gradient = jnp.dot(onehot, jnp.dot(by_bit_grad, onehot.T, precision=highest), precision=highest)
    empty_state = jnp.log(forward[0])
    distribution = forward.at[0].set(jnp.float32(0.0))
    return distribution, loglik, gradient, empty_state
```

```python
import jax
import jax.numpy as jnp
from jax import lax
from jax.experimental import pallas as pl
from jax.experimental.pallas import tpu as pltpu
from jax.sharding import PartitionSpec as P

MESH = pl.DeviceIdType.MESH
HIGH = lax.Precision.HIGHEST
F32 = jnp.float32

EVENTS = 25
PATIENTS = 256
LANES = 128
ROWS = 512
HALF = 256
CHUNK = 128
CHUNKS = 4
PIECE = 64
PIECES = 4
HOPS = 8
FIRST_DEVICE_BIT = 16
Z_BITS = ((20, 1), (21, 2), (22, 4), (23, 8))
CROSS = ((16, "grp", 1), (17, "grp", 2), (18, "grp", 4), (19, "grp", 8), (24, "wide", 16))
STAGES = (
    (((1,), ()),),
    (((2,), ()), ((), (16,)), ((2,), (16,))),
    (((4,), ()), ((8,), ()), ((4, 8), ())),
    (((), (1,)), ((), (2,)), ((), (1, 2))),
    (((), (4,)), ((), (8,)), ((), (4, 8))),
)
COLUMNS = EVENTS + 2
UP_ORDER = (0, 2, 1, 3)
DOWN_ORDER = (0, 1, 2, 3)


def nn(left, right):
    return lax.dot_general(
        left, right, (((1,), (0,)), ((), ())), precision=HIGH, preferred_element_type=F32
    )


def nt(left, right):
    return lax.dot_general(
        left, right, (((1,), (1,)), ((), ())), precision=HIGH, preferred_element_type=F32
    )


def iota(shape, axis):
    return lax.broadcasted_iota(jnp.int32, shape, axis)


def flip(index, distances):
    for distance in distances:
        index = index + distance - 2 * distance * ((index // distance) % 2)
    return index


def kernel(
    hazards_ref,
    order_ref,
    patients_ref,
    p_ref,
    q_ref,
    dist_ref,
    grad_ref,
    loglik_ref,
    empty_ref,
    rate,
    inverse,
    sum_f,
    sum_a,
    fwd,
    adj,
    counts,
    folded,
    ring_p,
    ring_q,
    ring_f,
    ring_a,
    cross_in,
    cross_half,
    reduce_out,
    reduce_in,
    onehot,
    hazards,
    tables,
    p_send,
    p_recv,
    q_send,
    q_recv,
    f_send,
    f_recv,
    a_send,
    a_recv,
    x_send,
    x_recv,
    h_send,
    h_recv,
    r_send,
    r_recv,
):
    wide = lax.axis_index("wide")
    grp = lax.axis_index("grp")
    device = wide * 16 + grp
    place = wide % 16
    above = {"wide": wide - place + (place + 1) % 16}
    below = {"wide": wide - place + (place + 15) % 16}

    def device_bit(bit):
        return (device // 2 ** (bit - FIRST_DEVICE_BIT)) % 2

    def partner(axis, distance):
        return {axis: flip(grp if axis == "grp" else wide, (distance,))}

    def remote(source, target, send, receive, where):
        return pltpu.make_async_remote_copy(
            src_ref=source,
            dst_ref=target,
            send_sem=send,
            recv_sem=receive,
            device_id=where,
            device_id_type=MESH,
        )

    barrier = pltpu.get_barrier_semaphore()
    neighbours = [above, below] + [partner(axis, distance) for _, axis, distance in CROSS]
    for neighbour in neighbours:
        pl.semaphore_signal(barrier, inc=1, device_id=neighbour, device_id_type=MESH)
    pl.semaphore_wait(barrier, len(neighbours))

    started = []

    def rows_of(chunk):
        return pl.ds(chunk * CHUNK, CHUNK)

    def up_copy(hop, chunk):
        rows = rows_of(chunk)
        source = p_ref.at[rows] if hop == 1 else ring_p.at[hop - 2, rows]
        return remote(
            source, ring_p.at[hop - 1, rows], p_send.at[hop - 1, chunk], p_recv.at[hop - 1, chunk], above
        )

    def down_copy(hop, chunk):
        rows = rows_of(chunk)
        source = q_ref.at[rows] if hop == 1 else ring_q.at[hop - 2, rows]
        return remote(
            source, ring_q.at[hop - 1, rows], q_send.at[hop - 1, chunk], q_recv.at[hop - 1, chunk], below
        )

    def up_half(hop, piece):
        rows = pl.ds(piece * PIECE, PIECE)
        if hop == 1:
            source = fwd.at[pl.ds(HALF + piece * PIECE, PIECE)]
        else:
            source = ring_f.at[hop - 2, rows]
        return remote(
            source, ring_f.at[hop - 1, rows], f_send.at[hop - 1, piece], f_recv.at[hop - 1, piece], above
        )

    def down_half(hop, piece):
        rows = pl.ds(piece * PIECE, PIECE)
        source = adj.at[rows] if hop == 1 else ring_a.at[hop - 2, rows]
        return remote(
            source, ring_a.at[hop - 1, rows], a_send.at[hop - 1, piece], a_recv.at[hop - 1, piece], below
        )

    def begin(copy):
        copy.start()
        started.append(copy)

    for up, down in zip(UP_ORDER, DOWN_ORDER):
        begin(up_copy(1, up))
        begin(down_copy(1, down))

    def cross_copy(number, source, target, send, receive):
        _, axis, distance = CROSS[number]
        return remote(
            source, target.at[number], send.at[number], receive.at[number], partner(axis, distance)
        )

    def cross_start(low, high, target, send, receive):
        for number, (bit, _, _) in enumerate(CROSS):
            for value, source in ((0, low), (1, high)):

                @pl.when(device_bit(bit) == value)
                def _():
                    cross_copy(number, source, target, send, receive).start()

            started.append(cross_copy(number, low, target, send, receive))

    cross_start(p_ref, q_ref, cross_in, x_send, x_recv)

    lane_id = iota((1, LANES), 1)
    lane_has = [((lane_id >> bit) & 1).astype(F32) for bit in range(7)]
    sub_id = iota((1, 8, LANES), 1)
    sub_has = [((sub_id >> bit) & 1).astype(F32) for bit in range(3)]

    def make_tables():
        lane8 = iota((8, LANES), 1)
        sub8 = iota((8, LANES), 0)
        hazards[...] = jnp.zeros_like(hazards)
        hazards[0:EVENTS, 0:EVENTS] = hazards_ref[...]
        onehot[...] = jnp.zeros_like(onehot)
        for tile in range(4):
            block = jnp.zeros((8, LANES), F32)
            for event in range(8 * tile, min(8 * tile + 8, EVENTS)):
                hit = (sub8 == event - 8 * tile) & (lane8 == order_ref[event])
                block = jnp.where(hit, 1.0, block)
            onehot[8 * tile : 8 * tile + 8, :] = block
        by_event = onehot[...]
        by_bit = by_event.T
        matrix = nn(by_bit, nn(hazards[...], by_event))
        square = (LANES, LANES)
        sub = iota(square, 0)
        lane = iota(square, 1)
        same = sub == lane
        diagonal = jnp.sum(jnp.where(same, matrix, 0.0), axis=1, keepdims=True)
        coupling = jnp.where(same, 0.0, matrix)
        lane_bits = jnp.where(sub < 7, (lane >> jnp.minimum(sub, 7)) & 1, 0).astype(F32)
        tables[ROWS : ROWS + 32, :] = jnp.exp(nn(coupling[0:32], lane_bits))
        row = iota((ROWS, LANES), 0)
        column = iota((ROWS, LANES), 1)
        row_bit = (row >> jnp.clip(column - 7, 0, 8)) & 1
        dev_bit = (device >> jnp.clip(column - FIRST_DEVICE_BIT, 0, 8)) & 1
        bits = jnp.where(column < 7, 0, jnp.where(column < 16, row_bit, dev_bit))
        features = jnp.where(column < EVENTS, bits, jnp.where(column == EVENTS, 1, 0)).astype(F32)
        widened = jnp.where(lane == EVENTS, diagonal, coupling)
        tables[0:ROWS, :] = jnp.exp(nt(features, widened))

    def make_rate(bit):
        def run():
            row_factor = tables[0:ROWS, bit : bit + 1]
            lane_factor = tables[ROWS + bit : ROWS + bit + 1, :]
            rate[bit] = row_factor * lane_factor

        return run

    def chunk_groups(values):
        return values.reshape(CHUNK // 8, 8, LANES)

    def lower_rows(values, distance):
        split = values.reshape(CHUNK // (2 * distance), 2, distance, LANES)
        low = split[:, 0:1]
        return jnp.concatenate([low, jnp.zeros_like(low)], axis=1).reshape(CHUNK, LANES)

    def make_inverse(chunk):
        def run():
            rows = rows_of(chunk)
            total = jnp.ones((CHUNK, LANES), F32)
            for bit in range(7):
                total = total + rate[bit, rows] * (1.0 - lane_has[bit])
            for bit in range(3):
                part = chunk_groups(rate[7 + bit, rows]) * (1.0 - sub_has[bit])
                total = total + part.reshape(CHUNK, LANES)
            for bit in range(4):
                total = total + lower_rows(rate[10 + bit, rows], 8 * 2**bit)
            if chunk % 2 == 0:
                total = total + rate[14, rows]
            if chunk < 2:
                total = total + rate[15, rows]
            for bit in range(FIRST_DEVICE_BIT, EVENTS):
                total = total + rate[bit, rows] * (1 - device_bit(bit)).astype(F32)
            inverse[rows] = 1.0 / total

        return run

    def local_forward(chunk):
        def run():
            rows = rows_of(chunk)
            values = p_ref[rows]
            total = jnp.zeros((CHUNK, LANES), F32)
            for bit in range(7):
                total = total + pltpu.roll(rate[bit, rows] * values, 2**bit, 1) * lane_has[bit]
            for bit in range(3):
                moved = pltpu.roll(chunk_groups(rate[7 + bit, rows] * values), 2**bit, 1)
                total = total + (moved * sub_has[bit]).reshape(CHUNK, LANES)
            for bit in range(4):
                distance = 8 * 2**bit
                split = (rate[10 + bit, rows] * values).reshape(
                    CHUNK // (2 * distance), 2, distance, LANES
                )
                low = split[:, 0:1]
                total = total + jnp.concatenate([jnp.zeros_like(low), low], axis=1).reshape(
                    CHUNK, LANES
                )
            if chunk % 2 == 1:
                other = rows_of(chunk - 1)
                total = total + rate[14, other] * p_ref[other]
            if chunk >= 2:
                other = rows_of(chunk - 2)
                total = total + rate[15, other] * p_ref[other]
            sum_f[rows] = total

        return run

    def local_adjoint(chunk):
        def run():
            rows = rows_of(chunk)
            values = q_ref[rows]
            total = jnp.zeros((CHUNK, LANES), F32)
            for bit in range(7):
                moved = pltpu.roll(values, LANES - 2**bit, 1)
                total = total + rate[bit, rows] * moved * (1.0 - lane_has[bit])
            grouped = chunk_groups(values)
            for bit in range(3):
                moved = pltpu.roll(grouped, 8 - 2**bit, 1) * (1.0 - sub_has[bit])
                total = total + rate[7 + bit, rows] * moved.reshape(CHUNK, LANES)
            for bit in range(4):
                distance = 8 * 2**bit
                split = values.reshape(CHUNK // (2 * distance), 2, distance, LANES)
                rates = rate[10 + bit, rows].reshape(split.shape)
                low = rates[:, 0:1] * split[:, 1:2]
                total = total + jnp.concatenate([low, jnp.zeros_like(low)], axis=1).reshape(
                    CHUNK, LANES
                )
            if chunk % 2 == 0:
                total = total + rate[14, rows] * q_ref[rows_of(chunk + 1)]
            if chunk < 2:
                total = total + rate[15, rows] * q_ref[rows_of(chunk + 2)]
            sum_a[rows] = total

        return run

    def make_counts():
        total = jnp.zeros((ROWS, LANES), F32)
        for part in range(PATIENTS // LANES):
            people = patients_ref[part : part + 1, :]
            state = jnp.zeros((1, LANES), jnp.int32)
            for event in range(EVENTS):
                state = state + (((people >> event) & 1) << order_ref[event])
            here = (state >> 16) == device
            row = jnp.where(here, (state >> 7) & (ROWS - 1), -1)
            lane = state & (LANES - 1)
            in_row = jnp.where(iota((ROWS, LANES), 0) == row, 1.0, 0.0)
            in_lane = jnp.where(iota((LANES, LANES), 0) == lane, 1.0, 0.0)
            total = total + lax.dot_general(
                in_row.astype(jnp.bfloat16),
                in_lane.astype(jnp.bfloat16),
                (((1,), (1,)), ((), ())),
                preferred_element_type=F32,
            )
        counts[...] = total

    def add_pair(bit, up, down):
        has = device_bit(bit).astype(F32)
        sum_f[...] += rate[bit] * up[...] * has
        sum_a[...] += rate[bit] * down[...] * (1.0 - has)

    def add_cross(number):
        def run():
            bit = CROSS[number][0]
            cross_copy(number, p_ref, cross_in, x_send, x_recv).wait_recv()
            add_pair(bit, cross_in.at[number], cross_in.at[number])

        return run

    def add_ring(bit, hop):
        def run():
            add_pair(bit, ring_p.at[hop - 1], ring_q.at[hop - 1])

        return run

    tasks = [make_tables]
    tasks += [make_rate(bit) for bit in range(EVENTS)]
    tasks += [make_counts]
    for chunk in range(CHUNKS):
        tasks += [make_inverse(chunk), local_forward(chunk), local_adjoint(chunk)]
    tasks += [add_cross(number) for number in range(len(CROSS))]
    tasks += [add_ring(20, 1), add_ring(21, 2)]
    slots = (HOPS - 1) * CHUNKS
    late = {5 * CHUNKS: add_ring(22, 4)}
    done = 0
    for hop in range(1, HOPS):
        for step, (up, down) in enumerate(zip(UP_ORDER, DOWN_ORDER)):
            slot = (hop - 1) * CHUNKS + step
            goal = -(-len(tasks) * (slot + 1) // (slots - CHUNKS))
            while done < min(goal, len(tasks)):
                tasks[done]()
                done += 1
            if slot in late:
                late[slot]()
            up_copy(hop, up).wait_recv()
            begin(up_copy(hop + 1, up))
            down_copy(hop, down).wait_recv()
            begin(down_copy(hop + 1, down))

    first_device = device == 0

    def finish_forward(chunk):
        rows = rows_of(chunk)
        has = device_bit(23).astype(F32)
        total = sum_f[rows] + rate[23, rows] * ring_p[HOPS - 1, rows] * has
        if chunk == 0:
            spot = (iota((CHUNK, LANES), 0) == 0) & (iota((CHUNK, LANES), 1) == 0) & first_device
            total = total + jnp.where(spot, float(2**EVENTS), 0.0)
            values = total * inverse[rows]
            dist_ref[rows] = jnp.where(spot, 0.0, values)
        else:
            values = total * inverse[rows]
            dist_ref[rows] = values
        fwd[rows] = values

    def finish_adjoint(chunk):
        rows = rows_of(chunk)
        lacks = 1.0 - device_bit(23).astype(F32)
        total = sum_a[rows] + rate[23, rows] * ring_q[HOPS - 1, rows] * lacks
        weights = counts[rows] / (float(PATIENTS) * fwd[rows])
        adj[rows] = (weights + total * 2.0**-12) * inverse[rows]

    for step, (up, down) in enumerate(zip(UP_ORDER, DOWN_ORDER)):
        up_copy(HOPS, up).wait_recv()
        finish_forward(up)
        if up >= 2:
            for piece in (2 * up - 4, 2 * up - 3):
                begin(up_half(1, piece))
        down_copy(HOPS, down).wait_recv()
        ready = [c for c in DOWN_ORDER[: step + 1] if c in UP_ORDER[: step + 1]]
        before = [c for c in DOWN_ORDER[:step] if c in UP_ORDER[:step]]
        for chunk in ready:
            if chunk not in before:
                finish_adjoint(chunk)
                if chunk < 2:
                    for piece in (2 * chunk, 2 * chunk + 1):
                        begin(down_half(1, piece))

    upper = pl.ds(HALF, HALF)
    lower = pl.ds(0, HALF)
    cross_start(fwd.at[upper], adj.at[lower], cross_half, h_send, h_recv)

    def put(column, total, parts):
        at = pl.ds(column * LANES, LANES)
        folded[0:8, at] = total
        for bit in range(6):
            folded[8 * bit + 8 : 8 * bit + 16, at] = parts[bit]

    def fold(values, bits):
        zero = jnp.zeros((8, LANES), F32)
        parts = [zero] * 6
        rest = values
        for position in reversed(range(len(bits))):
            size = 2**position
            high = rest[size:]
            parts[bits[position]] = jnp.sum(high, axis=0)
            rest = rest[:size] + high
        return rest[0], parts

    every = (0, 1, 2, 3, 4, 5)

    def gradient_lane(bit):
        def run():
            values = adj[...]
            moved = pltpu.roll(values, LANES - 2**bit, 1)
            term = rate[bit] * fwd[...] * (moved - values) * (1.0 - lane_has[bit])
            put(bit, *fold(term.reshape(64, 8, LANES), every))

        return run

    def gradient_sub(bit):
        def run():
            values = adj[...].reshape(64, 8, LANES)
            moved = pltpu.roll(values, 8 - 2**bit, 1)
            scaled = (rate[7 + bit] * fwd[...]).reshape(64, 8, LANES)
            term = scaled * (moved - values) * (1.0 - sub_has[bit])
            put(7 + bit, *fold(term, every))

        return run

    def gradient_row(bit):
        def run():
            distance = 8 * 2**bit
            shape = (ROWS // (2 * distance), 2, distance, LANES)
            values = adj[...].reshape(shape)
            rates = rate[10 + bit].reshape(shape)
            forwards = fwd[...].reshape(shape)
            term = rates[:, 0] * forwards[:, 0] * (values[:, 1] - values[:, 0])
            others = tuple(other for other in every if other != bit)
            put(10 + bit, *fold(term.reshape(32, 8, LANES), others))

        return run

    def gradient_pair(bit, from_above, from_below):
        has = device_bit(bit).astype(F32)
        lacks = 1.0 - has
        low = rate[bit, lower] * fwd[lower] * (from_above - adj[lower]) * lacks
        theirs = has * from_below - lacks * fwd[upper]
        high = rate[bit, upper] * adj[upper] * theirs
        term = jnp.concatenate([low, high], axis=0)
        put(bit, *fold(term.reshape(64, 8, LANES), every))

    def gradient_cross(number):
        def run():
            bit = CROSS[number][0]
            cross_copy(number, fwd.at[upper], cross_half, h_send, h_recv).wait_recv()
            gradient_pair(bit, cross_half[number], cross_half[number])

        return run

    def gradient_ring(bit, hop):
        def run():
            gradient_pair(bit, ring_a[hop - 1], ring_f[hop - 1])

        return run

    def likelihood():
        zero = [jnp.zeros((8, LANES), F32)] * 6
        logs = counts[...] * jnp.log(fwd[...])
        put(EVENTS, jnp.sum(logs.reshape(64, 8, LANES), axis=0), zero)
        spot = (iota((8, LANES), 0) == 0) & (iota((8, LANES), 1) == 0) & first_device
        put(EVENTS + 1, jnp.where(spot, jnp.log(fwd[0:8]), 0.0), zero)

    sub32 = iota((32, LANES), 0)
    lane32 = iota((32, LANES), 1)
    picker_sub = iota((32, 56), 0)
    picker_lane = iota((32, 56), 1)
    on_total = picker_lane < 8
    sub_part = (picker_lane >> jnp.clip(picker_sub - 7, 0, 2)) & 1
    is_sub = (picker_sub >= 7) & (picker_sub < 10)
    is_row = (picker_sub >= 10) & (picker_sub < 16)
    row_part = (picker_lane >> 3) == picker_sub - 9
    picker = jnp.where(
        is_sub,
        jnp.where(on_total, sub_part, 0),
        jnp.where(is_row, row_part.astype(jnp.int32), on_total.astype(jnp.int32)),
    ).astype(F32)
    lane_part = (lane32 >> jnp.minimum(sub32, 6)) & 1
    device_part = (device >> jnp.clip(sub32 - FIRST_DEVICE_BIT, 0, 8)) & 1
    weights32 = jnp.where(
        sub32 < 7,
        lane_part,
        jnp.where(sub32 < 16, 1, jnp.where(sub32 < EVENTS, device_part, (sub32 == EVENTS).astype(jnp.int32))),
    ).astype(F32)
    lane8 = iota((8, LANES), 1)

    def collect(columns):
        def run():
            tile = reduce_out[0]
            for column in columns:
                at = pl.ds(column * LANES, LANES)
                picked = nn(picker, folded[:, at]) * weights32
                sums = jnp.sum(jnp.where(sub32 == column, 0.0, picked) if column < EVENTS else picked, axis=1, keepdims=True)
                for group in range(4):
                    tile = jnp.where(
                        lane8 == 32 * group + column, sums[8 * group : 8 * group + 8], tile
                    )
            reduce_out[0] = tile

        return run

    reduce_out[0] = jnp.zeros((8, LANES), F32)
    tasks = [gradient_lane(bit) for bit in range(7)]
    tasks += [gradient_sub(bit) for bit in range(3)]
    tasks += [gradient_row(bit) for bit in range(6)]
    tasks += [likelihood]
    tasks += [gradient_cross(number) for number in range(len(CROSS))]
    tasks += [collect((column,)) for column in range(16)]
    tasks += [collect((column,)) for column in (16, 17, 18, 19, 24, 25, 26)]
    tasks += [gradient_ring(20, 1), gradient_ring(21, 2), collect((20,)), collect((21,))]
    late = {6 * PIECES: gradient_ring(22, 4), 6 * PIECES + 1: collect((22,))}
    slots = (HOPS - 1) * PIECES
    done = 0
    for hop in range(1, HOPS + 1):
        for piece in range(PIECES):
            slot = (hop - 1) * PIECES + piece
            goal = -(-len(tasks) * (slot + 1) // (slots - PIECES))
            while done < min(goal, len(tasks)):
                tasks[done]()
                done += 1
            if slot in late:
                late[slot]()
            up_half(hop, piece).wait_recv()
            if hop < HOPS:
                begin(up_half(hop + 1, piece))
            down_half(hop, piece).wait_recv()
            if hop < HOPS:
                begin(down_half(hop + 1, piece))
    gradient_ring(23, 8)()
    collect((23,))()

    for stage, peers in enumerate(STAGES):
        copies = []
        for number, (grp_distances, wide_distances) in enumerate(peers):
            where = {"grp": flip(grp, grp_distances), "wide": flip(wide, wide_distances)}
            copy = remote(
                reduce_out.at[stage],
                reduce_in.at[stage, number],
                r_send.at[stage, number],
                r_recv.at[stage, number],
                where,
            )
            begin(copy)
            copies.append(copy)
        for copy in copies:
            copy.wait_recv()
        total = reduce_out[stage] + reduce_in[stage, 0]
        if len(peers) == 3:
            total = total + (reduce_in[stage, 1] + reduce_in[stage, 2])
        reduce_out[stage + 1] = total

    tile = reduce_out[len(STAGES)]
    spread = jnp.concatenate(
        [tile] + [pltpu.roll(tile, LANES - 32 * group, 1) for group in range(1, 4)], axis=0
    )
    totals = spread[EVENTS : EVENTS + 1, :]
    inside = (sub32 < EVENTS) & (lane32 < EVENTS)
    matrix = jnp.where(inside, spread, 0.0)
    matrix = matrix + jnp.where(inside & (sub32 == lane32), totals, 0.0)
    matrix = jnp.concatenate([matrix, jnp.zeros((LANES - 32, LANES), F32)], axis=0)
    by_event = onehot[...]
    gradient = nt(nt(by_event[0:32], matrix), by_event)
    grad_ref[...] = gradient[0:EVENTS, 0:EVENTS]
    loglik_ref[0, 0] = jnp.sum(jnp.where((sub32 == EVENTS) & (lane32 == EVENTS), spread, 0.0)) / float(
        PATIENTS
    )
    empty_ref[0, 0] = jnp.sum(jnp.where((sub32 == EVENTS) & (lane32 == EVENTS + 1), spread, 0.0))

    for copy in started:
        copy.wait_send()


def body(log_hazards, bit_order, patients, start_dist, start_adjoint):
    vmem = pl.BlockSpec(memory_space=pltpu.VMEM)
    smem = pl.BlockSpec(memory_space=pltpu.SMEM)
    dma = pltpu.SemaphoreType.DMA

    def block(*shape):
        return pltpu.VMEM(shape, F32)

    distribution, gradient, loglik, empty_state = pl.pallas_call(
        kernel,
        out_shape=(
            jax.ShapeDtypeStruct((ROWS, LANES), F32),
            jax.ShapeDtypeStruct((EVENTS, EVENTS), F32),
            jax.ShapeDtypeStruct((1, 1), F32),
            jax.ShapeDtypeStruct((1, 1), F32),
        ),
        in_specs=[vmem, smem, vmem, vmem, vmem],
        out_specs=(vmem, vmem, smem, smem),
        scratch_shapes=[
            block(EVENTS, ROWS, LANES),
            block(ROWS, LANES),
            block(ROWS, LANES),
            block(ROWS, LANES),
            block(ROWS, LANES),
            block(ROWS, LANES),
            block(ROWS, LANES),
            block(56, COLUMNS * LANES),
            block(HOPS, ROWS, LANES),
            block(HOPS, ROWS, LANES),
            block(HOPS, HALF, LANES),
            block(HOPS, HALF, LANES),
            block(len(CROSS), ROWS, LANES),
            block(len(CROSS), HALF, LANES),
            block(len(STAGES) + 1, 8, LANES),
            block(len(STAGES), 3, 8, LANES),
            block(LANES, LANES),
            block(LANES, LANES),
            block(ROWS + 32, LANES),
            dma((HOPS, CHUNKS)),
            dma((HOPS, CHUNKS)),
            dma((HOPS, CHUNKS)),
            dma((HOPS, CHUNKS)),
            dma((HOPS, PIECES)),
            dma((HOPS, PIECES)),
            dma((HOPS, PIECES)),
            dma((HOPS, PIECES)),
            dma((len(CROSS),)),
            dma((len(CROSS),)),
            dma((len(CROSS),)),
            dma((len(CROSS),)),
            dma((len(STAGES), 3)),
            dma((len(STAGES), 3)),
        ],
        compiler_params=pltpu.CompilerParams(
            collective_id=0, has_side_effects=True, vmem_limit_bytes=48 * 2**20
        ),
    )(
        log_hazards,
        bit_order,
        patients.reshape(PATIENTS // LANES, LANES),
        start_dist.reshape(ROWS, LANES),
        start_adjoint.reshape(ROWS, LANES),
    )
    return distribution.reshape(-1), loglik.reshape(()), gradient, empty_state.reshape(())


def solution(mesh):
    return jax.shard_map(
        body,
        mesh=mesh,
        in_specs=(P(), P(), P(), P(("wide", "grp")), P(("wide", "grp"))),
        out_specs=(P(("wide", "grp")), P(), P(), P()),
        check_vma=False,
    )
```

```python
import jax
import jax.numpy as jnp
from jax import lax
from jax.experimental import pallas as pl
from jax.experimental.pallas import tpu as pltpu
from jax.sharding import PartitionSpec as P

MESH = pl.DeviceIdType.MESH
HIGH = lax.Precision.HIGHEST
F32 = jnp.float32

EVENTS = 25
PATIENTS = 256
LANES = 128
ROWS = 512
HALF = 256
CHUNK = 128
CHUNKS = 4
PIECES = 2
HOPS = 8
FIRST_DEVICE_BIT = 16
Z_BITS = ((20, 1), (21, 2), (22, 4), (23, 8))
CROSS = ((16, "grp", 1), (17, "grp", 2), (18, "grp", 4), (19, "grp", 8), (24, "wide", 16))
STAGES = (
    (((1,), ()),),
    (((2,), ()), ((), (16,)), ((2,), (16,))),
    (((4,), ()), ((8,), ()), ((4, 8), ())),
    tuple(((), tuple(2**bit for bit in range(4) if mask >> bit & 1)) for mask in range(1, 16)),
)
PEERS = max(len(peers) for peers in STAGES)
COLUMNS = EVENTS + 2
UP_ORDER = (0, 2, 1, 3)
DOWN_ORDER = (0, 1, 2, 3)


def nn(left, right):
    return lax.dot_general(
        left, right, (((1,), (0,)), ((), ())), precision=HIGH, preferred_element_type=F32
    )


def nt(left, right):
    return lax.dot_general(
        left, right, (((1,), (1,)), ((), ())), precision=HIGH, preferred_element_type=F32
    )


def iota(shape, axis):
    return lax.broadcasted_iota(jnp.int32, shape, axis)


def flip(index, distances):
    for distance in distances:
        index = index + distance - 2 * distance * ((index // distance) % 2)
    return index


def kernel(
    hazards_hbm,
    order_hbm,
    patients_hbm,
    p_hbm,
    q_hbm,
    dist_ref,
    grad_ref,
    loglik_ref,
    empty_ref,
    hazards_ref,
    order_ref,
    patients_ref,
    p_ref,
    q_ref,
    rate,
    inverse,
    sum_f,
    sum_a,
    fwd,
    adj,
    counts,
    folded,
    ring_p,
    ring_q,
    half_in,
    cross_in,
    cross_half,
    reduce_out,
    reduce_in,
    onehot,
    hazards,
    tables,
    p_send,
    p_recv,
    q_send,
    q_recv,
    z_send,
    z_recv,
    x_send,
    x_recv,
    h_send,
    h_recv,
    r_send,
    r_recv,
    local_sem,
):
    wide = lax.axis_index("wide")
    grp = lax.axis_index("grp")
    device = wide * 16 + grp
    place = wide % 16
    above = {"wide": wide - place + (place + 1) % 16}
    below = {"wide": wide - place + (place + 15) % 16}

    def device_bit(bit):
        return (device // 2 ** (bit - FIRST_DEVICE_BIT)) % 2

    def partner(axis, distance):
        return {axis: flip(grp if axis == "grp" else wide, (distance,))}

    def remote(source, target, send, receive, where):
        return pltpu.make_async_remote_copy(
            src_ref=source,
            dst_ref=target,
            send_sem=send,
            recv_sem=receive,
            device_id=where,
            device_id_type=MESH,
        )

    local_copies = [
        pltpu.make_async_copy(source, target, local_sem.at[number])
        for number, (source, target) in enumerate(
            (
                (hazards_hbm, hazards_ref),
                (order_hbm, order_ref),
                (patients_hbm, patients_ref),
                (p_hbm, p_ref),
                (q_hbm, q_ref),
            )
        )
    ]
    for copy in local_copies:
        copy.start()

    barrier = pltpu.get_barrier_semaphore()
    neighbours = [above, below] + [partner(axis, distance) for _, axis, distance in CROSS]
    for neighbour in neighbours:
        pl.semaphore_signal(barrier, inc=1, device_id=neighbour, device_id_type=MESH)
    pl.semaphore_wait(barrier, len(neighbours))

    started = []

    def rows_of(chunk):
        return pl.ds(chunk * CHUNK, CHUNK)

    def up_copy(hop, chunk):
        rows = rows_of(chunk)
        source = p_hbm.at[rows] if hop == 1 else ring_p.at[hop - 2, rows]
        return remote(
            source, ring_p.at[hop - 1, rows], p_send.at[hop - 1, chunk], p_recv.at[hop - 1, chunk], above
        )

    def down_copy(hop, chunk):
        rows = rows_of(chunk)
        source = q_hbm.at[rows] if hop == 1 else ring_q.at[hop - 2, rows]
        return remote(
            source, ring_q.at[hop - 1, rows], q_send.at[hop - 1, chunk], q_recv.at[hop - 1, chunk], below
        )

    odd = place % 2
    step_up = 2 * odd - 1

    def z_rows(piece):
        return pl.ds(piece * CHUNK, CHUNK)

    def z_copy(source, bit, piece, send, offset):
        return remote(
            source,
            half_in.at[bit, z_rows(piece)],
            z_send.at[send, piece],
            z_recv.at[bit, piece],
            {"wide": wide - place + (place + offset + 16) % 16},
        )

    guarded = []

    def begin_if(condition, copy):
        @pl.when(condition)
        def _():
            copy.start()

        guarded.append((condition, copy))

    def forward_piece(piece):
        return fwd.at[pl.ds(HALF + piece * CHUNK, CHUNK)]

    def adjoint_piece(piece):
        return adj.at[z_rows(piece)]

    def differs(bit):
        return (place // 2**bit) % 2 != odd

    def send_forward(piece):
        source = forward_piece(piece)
        begin_if(odd == 0, z_copy(source, 0, piece, 0, 1))
        begin_if((place // 8) % 2 == 0, z_copy(source, 3, piece, 1, 8))
        for bit in (2, 1):
            begin_if(differs(bit) & (odd == 1), z_copy(source, bit, piece, 1 + bit, 2**bit))

    def send_adjoint(piece):
        source = adjoint_piece(piece)
        begin_if(odd == 1, z_copy(source, 0, piece, 0, -1))
        begin_if((place // 8) % 2 == 1, z_copy(source, 3, piece, 1, -8))
        for bit in (2, 1):
            begin_if(differs(bit) & (odd == 0), z_copy(source, bit, piece, 1 + bit, -(2**bit)))

    def relay(piece):
        source = half_in.at[0, z_rows(piece)]
        for bit in (2, 1):
            begin_if(
                differs(bit), z_copy(source, bit, piece, 3 + bit, step_up * (2**bit - 1))
            )

    def z_wait(bit, piece):
        z_copy(adjoint_piece(piece), bit, piece, 0, 1).wait_recv()

    def begin(copy):
        copy.start()
        started.append(copy)

    for up, down in zip(UP_ORDER, DOWN_ORDER):
        begin(up_copy(1, up))
        begin(down_copy(1, down))

    def cross_copy(number, source, target, send, receive):
        _, axis, distance = CROSS[number]
        return remote(
            source, target.at[number], send.at[number], receive.at[number], partner(axis, distance)
        )

    def cross_start(low, high, target, send, receive):
        for number, (bit, _, _) in enumerate(CROSS):
            for value, source in ((0, low), (1, high)):

                @pl.when(device_bit(bit) == value)
                def _():
                    cross_copy(number, source, target, send, receive).start()

            started.append(cross_copy(number, low, target, send, receive))

    cross_start(p_hbm, q_hbm, cross_in, x_send, x_recv)

    lane_id = iota((1, LANES), 1)
    lane_has = [((lane_id >> bit) & 1).astype(F32) for bit in range(7)]
    sub_id = iota((1, 8, LANES), 1)
    sub_has = [((sub_id >> bit) & 1).astype(F32) for bit in range(3)]

    def make_tables():
        lane8 = iota((8, LANES), 1)
        sub8 = iota((8, LANES), 0)
        hazards[...] = jnp.zeros_like(hazards)
        hazards[0:EVENTS, 0:EVENTS] = hazards_ref[...]
        onehot[...] = jnp.zeros_like(onehot)
        for tile in range(4):
            block = jnp.zeros((8, LANES), F32)
            for event in range(8 * tile, min(8 * tile + 8, EVENTS)):
                hit = (sub8 == event - 8 * tile) & (lane8 == order_ref[event])
                block = jnp.where(hit, 1.0, block)
            onehot[8 * tile : 8 * tile + 8, :] = block
        by_event = onehot[...]
        by_bit = by_event.T
        matrix = nn(by_bit, nn(hazards[...], by_event))
        square = (LANES, LANES)
        sub = iota(square, 0)
        lane = iota(square, 1)
        same = sub == lane
        diagonal = jnp.sum(jnp.where(same, matrix, 0.0), axis=1, keepdims=True)
        coupling = jnp.where(same, 0.0, matrix)
        lane_bits = jnp.where(sub < 7, (lane >> jnp.minimum(sub, 7)) & 1, 0).astype(F32)
        tables[ROWS : ROWS + 32, :] = jnp.exp(nn(coupling[0:32], lane_bits))
        row = iota((ROWS, LANES), 0)
        column = iota((ROWS, LANES), 1)
        row_bit = (row >> jnp.clip(column - 7, 0, 8)) & 1
        dev_bit = (device >> jnp.clip(column - FIRST_DEVICE_BIT, 0, 8)) & 1
        bits = jnp.where(column < 7, 0, jnp.where(column < 16, row_bit, dev_bit))
        features = jnp.where(column < EVENTS, bits, jnp.where(column == EVENTS, 1, 0)).astype(F32)
        widened = jnp.where(lane == EVENTS, diagonal, coupling)
        tables[0:ROWS, :] = jnp.exp(nt(features, widened))

    def make_rate(bit):
        def run():
            row_factor = tables[0:ROWS, bit : bit + 1]
            lane_factor = tables[ROWS + bit : ROWS + bit + 1, :]
            rate[bit] = row_factor * lane_factor

        return run

    def chunk_groups(values):
        return values.reshape(CHUNK // 8, 8, LANES)

    def lower_rows(values, distance):
        split = values.reshape(CHUNK // (2 * distance), 2, distance, LANES)
        low = split[:, 0:1]
        return jnp.concatenate([low, jnp.zeros_like(low)], axis=1).reshape(CHUNK, LANES)

    def make_inverse(chunk):
        def run():
            rows = rows_of(chunk)
            total = jnp.ones((CHUNK, LANES), F32)
            for bit in range(7):
                total = total + rate[bit, rows] * (1.0 - lane_has[bit])
            for bit in range(3):
                part = chunk_groups(rate[7 + bit, rows]) * (1.0 - sub_has[bit])
                total = total + part.reshape(CHUNK, LANES)
            for bit in range(4):
                total = total + lower_rows(rate[10 + bit, rows], 8 * 2**bit)
            if chunk % 2 == 0:
                total = total + rate[14, rows]
            if chunk < 2:
                total = total + rate[15, rows]
            for bit in range(FIRST_DEVICE_BIT, EVENTS):
                total = total + rate[bit, rows] * (1 - device_bit(bit)).astype(F32)
            inverse[rows] = 1.0 / total

        return run

    def local_forward(chunk):
        def run():
            rows = rows_of(chunk)
            values = p_ref[rows]
            total = jnp.zeros((CHUNK, LANES), F32)
            for bit in range(7):
                total = total + pltpu.roll(rate[bit, rows] * values, 2**bit, 1) * lane_has[bit]
            for bit in range(3):
                moved = pltpu.roll(chunk_groups(rate[7 + bit, rows] * values), 2**bit, 1)
                total = total + (moved * sub_has[bit]).reshape(CHUNK, LANES)
            for bit in range(4):
                distance = 8 * 2**bit
                split = (rate[10 + bit, rows] * values).reshape(
                    CHUNK // (2 * distance), 2, distance, LANES
                )
                low = split[:, 0:1]
                total = total + jnp.concatenate([jnp.zeros_like(low), low], axis=1).reshape(
                    CHUNK, LANES
                )
            if chunk % 2 == 1:
                other = rows_of(chunk - 1)
                total = total + rate[14, other] * p_ref[other]
            if chunk >= 2:
                other = rows_of(chunk - 2)
                total = total + rate[15, other] * p_ref[other]
            sum_f[rows] = total

        return run

    def local_adjoint(chunk):
        def run():
            rows = rows_of(chunk)
            values = q_ref[rows]
            total = jnp.zeros((CHUNK, LANES), F32)
            for bit in range(7):
                moved = pltpu.roll(values, LANES - 2**bit, 1)
                total = total + rate[bit, rows] * moved * (1.0 - lane_has[bit])
            grouped = chunk_groups(values)
            for bit in range(3):
                moved = pltpu.roll(grouped, 8 - 2**bit, 1) * (1.0 - sub_has[bit])
                total = total + rate[7 + bit, rows] * moved.reshape(CHUNK, LANES)
            for bit in range(4):
                distance = 8 * 2**bit
                split = values.reshape(CHUNK // (2 * distance), 2, distance, LANES)
                rates = rate[10 + bit, rows].reshape(split.shape)
                low = rates[:, 0:1] * split[:, 1:2]
                total = total + jnp.concatenate([low, jnp.zeros_like(low)], axis=1).reshape(
                    CHUNK, LANES
                )
            if chunk % 2 == 0:
                total = total + rate[14, rows] * q_ref[rows_of(chunk + 1)]
            if chunk < 2:
                total = total + rate[15, rows] * q_ref[rows_of(chunk + 2)]
            sum_a[rows] = total

        return run

    def make_counts():
        total = jnp.zeros((ROWS, LANES), F32)
        for part in range(PATIENTS // LANES):
            people = patients_ref[part : part + 1, :]
            state = jnp.zeros((1, LANES), jnp.int32)
            for event in range(EVENTS):
                state = state + (((people >> event) & 1) << order_ref[event])
            here = (state >> 16) == device
            row = jnp.where(here, (state >> 7) & (ROWS - 1), -1)
            lane = state & (LANES - 1)
            in_row = jnp.where(iota((ROWS, LANES), 0) == row, 1.0, 0.0)
            in_lane = jnp.where(iota((LANES, LANES), 0) == lane, 1.0, 0.0)
            total = total + lax.dot_general(
                in_row.astype(jnp.bfloat16),
                in_lane.astype(jnp.bfloat16),
                (((1,), (1,)), ((), ())),
                preferred_element_type=F32,
            )
        counts[...] = total

    def add_pair(bit, up, down):
        has = device_bit(bit).astype(F32)
        sum_f[...] += rate[bit] * up[...] * has
        sum_a[...] += rate[bit] * down[...] * (1.0 - has)

    def add_cross(number):
        def run():
            bit = CROSS[number][0]
            cross_copy(number, p_hbm, cross_in, x_send, x_recv).wait_recv()
            add_pair(bit, cross_in.at[number], cross_in.at[number])

        return run

    def add_ring(bit, hop):
        def run():
            add_pair(bit, ring_p.at[hop - 1], ring_q.at[hop - 1])

        return run

    def land():
        for copy in local_copies:
            copy.wait()

    tasks = [land, make_tables]
    tasks += [make_rate(bit) for bit in range(EVENTS)]
    tasks += [make_counts]
    for chunk in range(CHUNKS):
        tasks += [make_inverse(chunk), local_forward(chunk), local_adjoint(chunk)]
    tasks += [add_cross(number) for number in range(len(CROSS))]
    tasks += [add_ring(20, 1), add_ring(21, 2)]
    slots = (HOPS - 1) * CHUNKS
    late = {5 * CHUNKS: add_ring(22, 4)}
    done = 0
    for hop in range(1, HOPS):
        for step, (up, down) in enumerate(zip(UP_ORDER, DOWN_ORDER)):
            slot = (hop - 1) * CHUNKS + step
            goal = -(-len(tasks) * (slot + 1) // (slots - CHUNKS))
            while done < min(goal, len(tasks)):
                tasks[done]()
                done += 1
            if slot in late:
                late[slot]()
            up_copy(hop, up).wait_recv()
            begin(up_copy(hop + 1, up))
            down_copy(hop, down).wait_recv()
            begin(down_copy(hop + 1, down))

    first_device = device == 0

    def finish_forward(chunk):
        rows = rows_of(chunk)
        has = device_bit(23).astype(F32)
        total = sum_f[rows] + rate[23, rows] * ring_p[HOPS - 1, rows] * has
        if chunk == 0:
            spot = (iota((CHUNK, LANES), 0) == 0) & (iota((CHUNK, LANES), 1) == 0) & first_device
            total = total + jnp.where(spot, float(2**EVENTS), 0.0)
            values = total * inverse[rows]
            dist_ref[rows] = jnp.where(spot, 0.0, values)
        else:
            values = total * inverse[rows]
            dist_ref[rows] = values
        fwd[rows] = values

    def finish_adjoint(chunk):
        rows = rows_of(chunk)
        lacks = 1.0 - device_bit(23).astype(F32)
        total = sum_a[rows] + rate[23, rows] * ring_q[HOPS - 1, rows] * lacks
        weights = counts[rows] / (float(PATIENTS) * fwd[rows])
        adj[rows] = (weights + total * 2.0**-12) * inverse[rows]

    for step, (up, down) in enumerate(zip(UP_ORDER, DOWN_ORDER)):
        up_copy(HOPS, up).wait_recv()
        finish_forward(up)
        if up >= 2:
            send_forward(up - 2)
        down_copy(HOPS, down).wait_recv()
        ready = [c for c in DOWN_ORDER[: step + 1] if c in UP_ORDER[: step + 1]]
        before = [c for c in DOWN_ORDER[:step] if c in UP_ORDER[:step]]
        for chunk in ready:
            if chunk not in before:
                finish_adjoint(chunk)
                if chunk < 2:
                    send_adjoint(chunk)

    upper = pl.ds(HALF, HALF)
    lower = pl.ds(0, HALF)
    cross_start(fwd.at[upper], adj.at[lower], cross_half, h_send, h_recv)

    def put(column, total, parts):
        at = pl.ds(column * LANES, LANES)
        folded[0:8, at] = total
        for bit in range(6):
            folded[8 * bit + 8 : 8 * bit + 16, at] = parts[bit]

    def fold(values, bits):
        zero = jnp.zeros((8, LANES), F32)
        parts = [zero] * 6
        rest = values
        for position in reversed(range(len(bits))):
            size = 2**position
            high = rest[size:]
            parts[bits[position]] = jnp.sum(high, axis=0)
            rest = rest[:size] + high
        return rest[0], parts

    every = (0, 1, 2, 3, 4, 5)

    def gradient_lane(bit):
        def run():
            values = adj[...]
            moved = pltpu.roll(values, LANES - 2**bit, 1)
            term = rate[bit] * fwd[...] * (moved - values) * (1.0 - lane_has[bit])
            put(bit, *fold(term.reshape(64, 8, LANES), every))

        return run

    def gradient_sub(bit):
        def run():
            values = adj[...].reshape(64, 8, LANES)
            moved = pltpu.roll(values, 8 - 2**bit, 1)
            scaled = (rate[7 + bit] * fwd[...]).reshape(64, 8, LANES)
            term = scaled * (moved - values) * (1.0 - sub_has[bit])
            put(7 + bit, *fold(term, every))

        return run

    def gradient_row(bit):
        def run():
            distance = 8 * 2**bit
            shape = (ROWS // (2 * distance), 2, distance, LANES)
            values = adj[...].reshape(shape)
            rates = rate[10 + bit].reshape(shape)
            forwards = fwd[...].reshape(shape)
            term = rates[:, 0] * forwards[:, 0] * (values[:, 1] - values[:, 0])
            others = tuple(other for other in every if other != bit)
            put(10 + bit, *fold(term.reshape(32, 8, LANES), others))

        return run

    def gradient_pair(bit, from_above, from_below):
        has = device_bit(bit).astype(F32)
        lacks = 1.0 - has
        low = rate[bit, lower] * fwd[lower] * (from_above - adj[lower]) * lacks
        theirs = has * from_below - lacks * fwd[upper]
        high = rate[bit, upper] * adj[upper] * theirs
        term = jnp.concatenate([low, high], axis=0)
        put(bit, *fold(term.reshape(64, 8, LANES), every))

    def gradient_cross(number):
        def run():
            bit = CROSS[number][0]
            cross_copy(number, fwd.at[upper], cross_half, h_send, h_recv).wait_recv()
            gradient_pair(bit, cross_half[number], cross_half[number])

        return run

    def gradient_ring(bit):
        def run():
            if bit:
                for piece in range(PIECES):
                    z_wait(bit, piece)
            gradient_pair(20 + bit, half_in[bit], half_in[bit])

        return run

    def relay_all():
        for piece in range(PIECES):
            z_wait(0, piece)
            relay(piece)

    def likelihood():
        zero = [jnp.zeros((8, LANES), F32)] * 6
        logs = counts[...] * jnp.log(fwd[...])
        put(EVENTS, jnp.sum(logs.reshape(64, 8, LANES), axis=0), zero)
        spot = (iota((8, LANES), 0) == 0) & (iota((8, LANES), 1) == 0) & first_device
        put(EVENTS + 1, jnp.where(spot, jnp.log(fwd[0:8]), 0.0), zero)

    sub32 = iota((32, LANES), 0)
    lane32 = iota((32, LANES), 1)
    picker_sub = iota((32, 56), 0)
    picker_lane = iota((32, 56), 1)
    on_total = picker_lane < 8
    sub_part = (picker_lane >> jnp.clip(picker_sub - 7, 0, 2)) & 1
    is_sub = (picker_sub >= 7) & (picker_sub < 10)
    is_row = (picker_sub >= 10) & (picker_sub < 16)
    row_part = (picker_lane >> 3) == picker_sub - 9
    picker = jnp.where(
        is_sub,
        jnp.where(on_total, sub_part, 0),
        jnp.where(is_row, row_part.astype(jnp.int32), on_total.astype(jnp.int32)),
    ).astype(F32)
    lane_part = (lane32 >> jnp.minimum(sub32, 6)) & 1
    device_part = (device >> jnp.clip(sub32 - FIRST_DEVICE_BIT, 0, 8)) & 1
    weights32 = jnp.where(
        sub32 < 7,
        lane_part,
        jnp.where(sub32 < 16, 1, jnp.where(sub32 < EVENTS, device_part, (sub32 == EVENTS).astype(jnp.int32))),
    ).astype(F32)
    lane8 = iota((8, LANES), 1)

    def collect(columns):
        def run():
            tile = reduce_out[0]
            for column in columns:
                at = pl.ds(column * LANES, LANES)
                picked = nn(picker, folded[:, at]) * weights32
                sums = jnp.sum(jnp.where(sub32 == column, 0.0, picked) if column < EVENTS else picked, axis=1, keepdims=True)
                for group in range(4):
                    tile = jnp.where(
                        lane8 == 32 * group + column, sums[8 * group : 8 * group + 8], tile
                    )
            reduce_out[0] = tile

        return run

    reduce_out[0] = jnp.zeros((8, LANES), F32)
    tasks = [gradient_lane(bit) for bit in range(5)]
    tasks += [relay_all]
    tasks += [gradient_lane(bit) for bit in range(5, 7)]
    tasks += [gradient_sub(bit) for bit in range(3)]
    tasks += [gradient_row(bit) for bit in range(6)]
    tasks += [likelihood, gradient_ring(0)]
    tasks += [collect(tuple(range(16)) + (20, 25, 26))]
    tasks += [gradient_cross(number) for number in range(len(CROSS))]
    tasks += [collect((16, 17, 18, 19, 24))]
    for bit in (1, 2, 3):
        tasks += [gradient_ring(bit), collect((20 + bit,))]
    for task in tasks:
        task()

    for stage, peers in enumerate(STAGES):
        copies = []
        for number, (grp_distances, wide_distances) in enumerate(peers):
            where = {"grp": flip(grp, grp_distances), "wide": flip(wide, wide_distances)}
            copy = remote(
                reduce_out.at[stage],
                reduce_in.at[stage, number],
                r_send.at[stage, number],
                r_recv.at[stage, number],
                where,
            )
            begin(copy)
            copies.append(copy)
        for copy in copies:
            copy.wait_recv()
        parts = [reduce_out[stage]] + [reduce_in[stage, number] for number in range(len(peers))]
        while len(parts) > 1:
            parts = [low + high for low, high in zip(parts[0::2], parts[1::2])]
        reduce_out[stage + 1] = parts[0]

    tile = reduce_out[len(STAGES)]
    spread = jnp.concatenate(
        [tile] + [pltpu.roll(tile, LANES - 32 * group, 1) for group in range(1, 4)], axis=0
    )
    totals = spread[EVENTS : EVENTS + 1, :]
    inside = (sub32 < EVENTS) & (lane32 < EVENTS)
    matrix = jnp.where(inside, spread, 0.0)
    matrix = matrix + jnp.where(inside & (sub32 == lane32), totals, 0.0)
    matrix = jnp.concatenate([matrix, jnp.zeros((LANES - 32, LANES), F32)], axis=0)
    by_event = onehot[...]
    gradient = nt(nt(by_event[0:32], matrix), by_event)
    grad_ref[...] = gradient[0:EVENTS, 0:EVENTS]
    loglik_ref[0, 0] = jnp.sum(jnp.where((sub32 == EVENTS) & (lane32 == EVENTS), spread, 0.0)) / float(
        PATIENTS
    )
    empty_ref[0, 0] = jnp.sum(jnp.where((sub32 == EVENTS) & (lane32 == EVENTS + 1), spread, 0.0))

    for copy in started:
        copy.wait_send()
    for condition, copy in guarded:

        @pl.when(condition)
        def _():
            copy.wait_send()


def body(log_hazards, bit_order, patients, start_dist, start_adjoint):
    vmem = pl.BlockSpec(memory_space=pltpu.VMEM)
    smem = pl.BlockSpec(memory_space=pltpu.SMEM)
    dma = pltpu.SemaphoreType.DMA

    def block(*shape):
        return pltpu.VMEM(shape, F32)

    distribution, gradient, loglik, empty_state = pl.pallas_call(
        kernel,
        out_shape=(
            jax.ShapeDtypeStruct((ROWS, LANES), F32),
            jax.ShapeDtypeStruct((EVENTS, EVENTS), F32),
            jax.ShapeDtypeStruct((1, 1), F32),
            jax.ShapeDtypeStruct((1, 1), F32),
        ),
        in_specs=[pl.BlockSpec(memory_space=pl.ANY)] * 5,
        out_specs=(vmem, vmem, smem, smem),
        scratch_shapes=[
            block(EVENTS, EVENTS),
            pltpu.SMEM((EVENTS,), jnp.int32),
            pltpu.VMEM((PATIENTS // LANES, LANES), jnp.int32),
            block(ROWS, LANES),
            block(ROWS, LANES),
            block(EVENTS, ROWS, LANES),
            block(ROWS, LANES),
            block(ROWS, LANES),
            block(ROWS, LANES),
            block(ROWS, LANES),
            block(ROWS, LANES),
            block(ROWS, LANES),
            block(56, COLUMNS * LANES),
            block(HOPS, ROWS, LANES),
            block(HOPS, ROWS, LANES),
            block(4, HALF, LANES),
            block(len(CROSS), ROWS, LANES),
            block(len(CROSS), HALF, LANES),
            block(len(STAGES) + 1, 8, LANES),
            block(len(STAGES), PEERS, 8, LANES),
            block(LANES, LANES),
            block(LANES, LANES),
            block(ROWS + 32, LANES),
            dma((HOPS, CHUNKS)),
            dma((HOPS, CHUNKS)),
            dma((HOPS, CHUNKS)),
            dma((HOPS, CHUNKS)),
            dma((6, PIECES)),
            dma((4, PIECES)),
            dma((len(CROSS),)),
            dma((len(CROSS),)),
            dma((len(CROSS),)),
            dma((len(CROSS),)),
            dma((len(STAGES), PEERS)),
            dma((len(STAGES), PEERS)),
            dma((5,)),
        ],
        compiler_params=pltpu.CompilerParams(
            collective_id=0, has_side_effects=True, vmem_limit_bytes=60 * 2**20
        ),
    )(
        log_hazards,
        bit_order,
        patients.reshape(PATIENTS // LANES, LANES),
        start_dist.reshape(ROWS, LANES),
        start_adjoint.reshape(ROWS, LANES),
    )
    return distribution.reshape(-1), loglik.reshape(()), gradient, empty_state.reshape(())


def solution(mesh):
    return jax.shard_map(
        body,
        mesh=mesh,
        in_specs=(P(), P(), P(), P(("wide", "grp")), P(("wide", "grp"))),
        out_specs=(P(("wide", "grp")), P(), P(), P()),
        check_vma=False,
    )
```

```python
import jax
import jax.numpy as jnp
from jax import lax
from jax.experimental import pallas as pl
from jax.experimental.pallas import tpu as pltpu
from jax.sharding import PartitionSpec as P

MESH = pl.DeviceIdType.MESH
HIGH = lax.Precision.HIGHEST
F32 = jnp.float32

EVENTS = 25
PATIENTS = 256
LANES = 128
ROWS = 512
HALF = 256
CHUNK = 128
CHUNKS = 4
PIECES = 2
FIRST_DEVICE_BIT = 16
CROSS = ((16, "grp", 1), (17, "grp", 2), (18, "grp", 4), (19, "grp", 8), (24, "wide", 16))
STAGES = (
    (((1,), ()),),
    (((2,), ()), ((), (16,)), ((2,), (16,))),
    (((4,), ()), ((8,), ()), ((4, 8), ())),
    tuple(((), tuple(2**bit for bit in range(4) if mask >> bit & 1)) for mask in range(1, 16)),
)
PEERS = max(len(peers) for peers in STAGES)
COLUMNS = EVENTS + 2
ORDER = (0, 2, 1, 3)


def nn(left, right):
    return lax.dot_general(
        left, right, (((1,), (0,)), ((), ())), precision=HIGH, preferred_element_type=F32
    )


def nt(left, right):
    return lax.dot_general(
        left, right, (((1,), (1,)), ((), ())), precision=HIGH, preferred_element_type=F32
    )


def iota(shape, axis):
    return lax.broadcasted_iota(jnp.int32, shape, axis)


def flip(index, distances):
    for distance in distances:
        index = index + distance - 2 * distance * ((index // distance) % 2)
    return index


def kernel(
    hazards_hbm,
    order_hbm,
    patients_hbm,
    p_hbm,
    q_hbm,
    dist_ref,
    grad_ref,
    loglik_ref,
    empty_ref,
    hazards_ref,
    order_ref,
    patients_ref,
    p_ref,
    q_ref,
    rate,
    inverse,
    sum_f,
    sum_a,
    fwd,
    adj,
    counts,
    folded,
    z_in,
    merge_in,
    wrap_in,
    merged,
    factor,
    half_in,
    cross_in,
    cross_half,
    reduce_out,
    reduce_in,
    onehot,
    hazards,
    tables,
    p_send,
    p_recv,
    m_recv,
    z_send,
    z_recv,
    x_send,
    x_recv,
    h_send,
    h_recv,
    r_send,
    r_recv,
    local_sem,
):
    wide = lax.axis_index("wide")
    grp = lax.axis_index("grp")
    device = wide * 16 + grp
    place = wide % 16

    def to_place(offset):
        return {"wide": wide - place + (place + offset + 16) % 16}

    def device_bit(bit):
        return (device // 2 ** (bit - FIRST_DEVICE_BIT)) % 2

    def partner(axis, distance):
        return {axis: flip(grp if axis == "grp" else wide, (distance,))}

    def remote(source, target, send, receive, where):
        return pltpu.make_async_remote_copy(
            src_ref=source,
            dst_ref=target,
            send_sem=send,
            recv_sem=receive,
            device_id=where,
            device_id_type=MESH,
        )

    local_copies = [
        pltpu.make_async_copy(source, target, local_sem.at[number])
        for number, (source, target) in enumerate(
            (
                (hazards_hbm, hazards_ref),
                (order_hbm, order_ref),
                (patients_hbm, patients_ref),
                (p_hbm, p_ref),
                (q_hbm, q_ref),
            )
        )
    ]
    for copy in local_copies:
        copy.start()

    barrier = pltpu.get_barrier_semaphore()
    neighbours = [to_place(offset) for offset in (-4, -3, -2, -1, 1, 2, 3, 4)]
    neighbours += [partner(axis, distance) for _, axis, distance in CROSS]
    for neighbour in neighbours:
        pl.semaphore_signal(barrier, inc=1, device_id=neighbour, device_id_type=MESH)
    pl.semaphore_wait(barrier, len(neighbours))

    started = []

    def rows_of(chunk):
        return pl.ds(chunk * CHUNK, CHUNK)

    odd = place % 2
    step_up = 2 * odd - 1

    def z_rows(piece):
        return pl.ds(piece * CHUNK, CHUNK)

    def z_copy(source, bit, piece, send, offset):
        return remote(
            source,
            half_in.at[bit, z_rows(piece)],
            z_send.at[send, piece],
            z_recv.at[bit, piece],
            {"wide": wide - place + (place + offset + 16) % 16},
        )

    guarded = []

    def begin_if(condition, copy):
        @pl.when(condition)
        def _():
            copy.start()

        guarded.append((condition, copy))

    def forward_piece(piece):
        return fwd.at[pl.ds(HALF + piece * CHUNK, CHUNK)]

    def adjoint_piece(piece):
        return adj.at[z_rows(piece)]

    def differs(bit):
        return (place // 2**bit) % 2 != odd

    def send_forward(piece):
        source = forward_piece(piece)
        begin_if(odd == 0, z_copy(source, 0, piece, 0, 1))
        begin_if((place // 8) % 2 == 0, z_copy(source, 3, piece, 1, 8))
        for bit in (2, 1):
            begin_if(differs(bit) & (odd == 1), z_copy(source, bit, piece, 1 + bit, 2**bit))

    def send_adjoint(piece):
        source = adjoint_piece(piece)
        begin_if(odd == 1, z_copy(source, 0, piece, 0, -1))
        begin_if((place // 8) % 2 == 1, z_copy(source, 3, piece, 1, -8))
        for bit in (2, 1):
            begin_if(differs(bit) & (odd == 0), z_copy(source, bit, piece, 1 + bit, -(2**bit)))

    def relay(piece):
        source = half_in.at[0, z_rows(piece)]
        for bit in (2, 1):
            begin_if(
                differs(bit), z_copy(source, bit, piece, 3 + bit, step_up * (2**bit - 1))
            )

    def z_wait(bit, piece):
        z_copy(adjoint_piece(piece), bit, piece, 0, 1).wait_recv()

    def begin(copy):
        copy.start()
        started.append(copy)

    top = (place // 8) % 2
    middle = top != (place // 4) % 2
    end = top == (place // 4) % 2
    toward = 4 - 8 * top

    def first_copy(source, bit, chunk, send, offset):
        rows = rows_of(chunk)
        return remote(
            source, z_in.at[bit, rows], p_send.at[send, chunk], p_recv.at[bit, chunk], to_place(offset)
        )

    def first_wait(bit, chunk):
        first_copy(p_hbm.at[rows_of(chunk)], bit, chunk, 0, 1).wait_recv()

    def half_rows(chunk):
        return pl.ds((chunk % 2) * CHUNK, CHUNK)

    def first_leg(source, chunk, side):
        if chunk < 2:
            target, semaphore, offset = merge_in.at[half_rows(chunk)], m_recv.at[0, chunk], toward
        else:
            target, semaphore, offset = wrap_in.at[side, half_rows(chunk)], m_recv.at[side, chunk], -toward
        return remote(source, target, p_send.at[5, chunk], semaphore, to_place(offset))

    def start_far(chunk):
        rows = rows_of(chunk)
        for value, source in ((0, p_hbm.at[rows]), (1, q_hbm.at[rows])):
            ready = (top == value) & middle if chunk < 2 else top == value
            begin_if(ready, first_leg(source, chunk, value))

    def start_neighbour(chunk):
        rows = rows_of(chunk)
        begin_if(odd == 0, first_copy(p_hbm.at[rows], 0, chunk, 0, 1))
        begin_if(odd == 1, first_copy(q_hbm.at[rows], 0, chunk, 0, -1))

    def start_own(chunk):
        rows = rows_of(chunk)
        for bit in (2, 1):
            wanted = differs(bit) & end if bit == 2 and chunk < 2 else differs(bit)
            begin_if(wanted & (odd == 1), first_copy(p_hbm.at[rows], bit, chunk, bit, 2**bit))
            begin_if(wanted & (odd == 0), first_copy(q_hbm.at[rows], bit, chunk, bit, -(2**bit)))

    for chunk in ORDER:
        start_far(chunk)
    for chunk in ORDER:
        start_neighbour(chunk)
    for chunk in ORDER:
        start_own(chunk)

    def pass_neighbour(chunk):
        def run():
            first_wait(0, chunk)
            source = z_in.at[0, rows_of(chunk)]
            for bit in (2, 1):
                wanted = differs(bit) & end if bit == 2 and chunk < 2 else differs(bit)
                begin_if(wanted, first_copy(source, bit, chunk, 2 + bit, step_up * (2**bit - 1)))

        return run

    def pass_wrap(chunk):
        def run():
            rows = half_rows(chunk)
            for side, offset in ((0, -4), (1, 4)):
                source = wrap_in.at[side, rows]

                @pl.when(end)
                def _():
                    remote(
                        source, source, p_send.at[5, chunk], m_recv.at[side, chunk], to_place(4)
                    ).wait_recv()

                begin_if(end, first_copy(source, 3, chunk, 6 + side, offset))

        return run

    def pass_merged(chunk):
        def run():
            rows = rows_of(chunk)
            source = merge_in.at[rows]

            @pl.when(middle)
            def _():
                remote(source, source, p_send.at[5, chunk], m_recv.at[0, chunk], to_place(4)).wait_recv()
                high = top.astype(F32)
                own = high * p_ref[rows] + (1.0 - high) * q_ref[rows]
                far = rate[23, rows] * factor[0:1, :] * merge_in[rows]
                merged[rows] = far + rate[22, rows] * own

            begin_if(middle, first_copy(merged.at[rows], 2, chunk, 7, -toward))

        return run

    def pass_second(chunk):
        def run():
            first_wait(2, chunk)
            begin_if(middle, first_copy(z_in.at[2, rows_of(chunk)], 3, chunk, 6, toward))

        return run

    def cross_copy(number, source, target, send, receive):
        _, axis, distance = CROSS[number]
        return remote(
            source, target.at[number], send.at[number], receive.at[number], partner(axis, distance)
        )

    def cross_start(low, high, target, send, receive):
        for number, (bit, _, _) in enumerate(CROSS):
            for value, source in ((0, low), (1, high)):

                @pl.when(device_bit(bit) == value)
                def _():
                    cross_copy(number, source, target, send, receive).start()

            started.append(cross_copy(number, low, target, send, receive))

    cross_start(p_hbm, q_hbm, cross_in, x_send, x_recv)

    lane_id = iota((1, LANES), 1)
    lane_has = [((lane_id >> bit) & 1).astype(F32) for bit in range(7)]
    sub_id = iota((1, 8, LANES), 1)
    sub_has = [((sub_id >> bit) & 1).astype(F32) for bit in range(3)]

    def make_tables():
        lane8 = iota((8, LANES), 1)
        sub8 = iota((8, LANES), 0)
        hazards[...] = jnp.zeros_like(hazards)
        hazards[0:EVENTS, 0:EVENTS] = hazards_ref[...]
        onehot[...] = jnp.zeros_like(onehot)
        for tile in range(4):
            block = jnp.zeros((8, LANES), F32)
            for event in range(8 * tile, min(8 * tile + 8, EVENTS)):
                hit = (sub8 == event - 8 * tile) & (lane8 == order_ref[event])
                block = jnp.where(hit, 1.0, block)
            onehot[8 * tile : 8 * tile + 8, :] = block
        by_event = onehot[...]
        by_bit = by_event.T
        matrix = nn(by_bit, nn(hazards[...], by_event))
        square = (LANES, LANES)
        sub = iota(square, 0)
        lane = iota(square, 1)
        same = sub == lane
        diagonal = jnp.sum(jnp.where(same, matrix, 0.0), axis=1, keepdims=True)
        coupling = jnp.where(same, 0.0, matrix)
        sign = (2 * top - 1).astype(F32)
        factor[...] = jnp.broadcast_to(jnp.exp(coupling[23:24, 22:23] * sign), (8, LANES))
        lane_bits = jnp.where(sub < 7, (lane >> jnp.minimum(sub, 7)) & 1, 0).astype(F32)
        tables[ROWS : ROWS + 32, :] = jnp.exp(nn(coupling[0:32], lane_bits))
        row = iota((ROWS, LANES), 0)
        column = iota((ROWS, LANES), 1)
        row_bit = (row >> jnp.clip(column - 7, 0, 8)) & 1
        dev_bit = (device >> jnp.clip(column - FIRST_DEVICE_BIT, 0, 8)) & 1
        bits = jnp.where(column < 7, 0, jnp.where(column < 16, row_bit, dev_bit))
        features = jnp.where(column < EVENTS, bits, jnp.where(column == EVENTS, 1, 0)).astype(F32)
        widened = jnp.where(lane == EVENTS, diagonal, coupling)
        tables[0:ROWS, :] = jnp.exp(nt(features, widened))

    def make_rate(bit):
        def run():
            row_factor = tables[0:ROWS, bit : bit + 1]
            lane_factor = tables[ROWS + bit : ROWS + bit + 1, :]
            rate[bit] = row_factor * lane_factor

        return run

    def chunk_groups(values):
        return values.reshape(CHUNK // 8, 8, LANES)

    def lower_rows(values, distance):
        split = values.reshape(CHUNK // (2 * distance), 2, distance, LANES)
        low = split[:, 0:1]
        return jnp.concatenate([low, jnp.zeros_like(low)], axis=1).reshape(CHUNK, LANES)

    def make_inverse(chunk):
        def run():
            rows = rows_of(chunk)
            total = jnp.ones((CHUNK, LANES), F32)
            for bit in range(7):
                total = total + rate[bit, rows] * (1.0 - lane_has[bit])
            for bit in range(3):
                part = chunk_groups(rate[7 + bit, rows]) * (1.0 - sub_has[bit])
                total = total + part.reshape(CHUNK, LANES)
            for bit in range(4):
                total = total + lower_rows(rate[10 + bit, rows], 8 * 2**bit)
            if chunk % 2 == 0:
                total = total + rate[14, rows]
            if chunk < 2:
                total = total + rate[15, rows]
            for bit in range(FIRST_DEVICE_BIT, EVENTS):
                total = total + rate[bit, rows] * (1 - device_bit(bit)).astype(F32)
            inverse[rows] = 1.0 / total

        return run

    def local_forward(chunk):
        def run():
            rows = rows_of(chunk)
            values = p_ref[rows]
            total = jnp.zeros((CHUNK, LANES), F32)
            for bit in range(7):
                total = total + pltpu.roll(rate[bit, rows] * values, 2**bit, 1) * lane_has[bit]
            for bit in range(3):
                moved = pltpu.roll(chunk_groups(rate[7 + bit, rows] * values), 2**bit, 1)
                total = total + (moved * sub_has[bit]).reshape(CHUNK, LANES)
            for bit in range(4):
                distance = 8 * 2**bit
                split = (rate[10 + bit, rows] * values).reshape(
                    CHUNK // (2 * distance), 2, distance, LANES
                )
                low = split[:, 0:1]
                total = total + jnp.concatenate([jnp.zeros_like(low), low], axis=1).reshape(
                    CHUNK, LANES
                )
            if chunk % 2 == 1:
                other = rows_of(chunk - 1)
                total = total + rate[14, other] * p_ref[other]
            if chunk >= 2:
                other = rows_of(chunk - 2)
                total = total + rate[15, other] * p_ref[other]
            sum_f[rows] = total

        return run

    def local_adjoint(chunk):
        def run():
            rows = rows_of(chunk)
            values = q_ref[rows]
            total = jnp.zeros((CHUNK, LANES), F32)
            for bit in range(7):
                moved = pltpu.roll(values, LANES - 2**bit, 1)
                total = total + rate[bit, rows] * moved * (1.0 - lane_has[bit])
            grouped = chunk_groups(values)
            for bit in range(3):
                moved = pltpu.roll(grouped, 8 - 2**bit, 1) * (1.0 - sub_has[bit])
                total = total + rate[7 + bit, rows] * moved.reshape(CHUNK, LANES)
            for bit in range(4):
                distance = 8 * 2**bit
                split = values.reshape(CHUNK // (2 * distance), 2, distance, LANES)
                rates = rate[10 + bit, rows].reshape(split.shape)
                low = rates[:, 0:1] * split[:, 1:2]
                total = total + jnp.concatenate([low, jnp.zeros_like(low)], axis=1).reshape(
                    CHUNK, LANES
                )
            if chunk % 2 == 0:
                total = total + rate[14, rows] * q_ref[rows_of(chunk + 1)]
            if chunk < 2:
                total = total + rate[15, rows] * q_ref[rows_of(chunk + 2)]
            sum_a[rows] = total

        return run

    def make_counts():
        total = jnp.zeros((ROWS, LANES), F32)
        for part in range(PATIENTS // LANES):
            people = patients_ref[part : part + 1, :]
            state = jnp.zeros((1, LANES), jnp.int32)
            for event in range(EVENTS):
                state = state + (((people >> event) & 1) << order_ref[event])
            here = (state >> 16) == device
            row = jnp.where(here, (state >> 7) & (ROWS - 1), -1)
            lane = state & (LANES - 1)
            in_row = jnp.where(iota((ROWS, LANES), 0) == row, 1.0, 0.0)
            in_lane = jnp.where(iota((LANES, LANES), 0) == lane, 1.0, 0.0)
            total = total + lax.dot_general(
                in_row.astype(jnp.bfloat16),
                in_lane.astype(jnp.bfloat16),
                (((1,), (1,)), ((), ())),
                preferred_element_type=F32,
            )
        counts[...] = total

    def add_pair(bit, received):
        has = device_bit(bit).astype(F32)
        term = rate[bit] * received[...]
        sum_f[...] += term * has
        sum_a[...] += term * (1.0 - has)

    def add_cross(number):
        def run():
            bit = CROSS[number][0]
            cross_copy(number, p_hbm, cross_in, x_send, x_recv).wait_recv()
            add_pair(bit, cross_in.at[number])

        return run

    def land():
        for copy in local_copies:
            copy.wait()

    def add_first():
        for chunk in ORDER:
            first_wait(1, chunk)
        add_pair(20, z_in.at[0])
        add_pair(21, z_in.at[1])

    @pl.when(end)
    def _():
        z_in[3, 0:HALF] = jnp.zeros((HALF, LANES), F32)

    tasks = [land, make_tables, make_rate(22), make_rate(23)]
    tasks += [make_rate(bit) for bit in range(EVENTS) if bit not in (22, 23)]
    tasks += [make_counts]
    for chunk in range(CHUNKS):
        tasks += [make_inverse(chunk), local_forward(chunk), local_adjoint(chunk)]
    tasks += [add_cross(number) for number in range(len(CROSS))]
    services = [
        pass_wrap(2),
        pass_merged(0),
        pass_wrap(3),
        pass_merged(1),
        pass_neighbour(0),
        pass_neighbour(2),
        pass_neighbour(1),
        pass_neighbour(3),
        pass_second(0),
        pass_second(1),
    ]
    done = 0
    for number, service in enumerate(services):
        goal = max(6, len(tasks) * (number + 1) // (len(services) + 1))
        while done < goal:
            tasks[done]()
            done += 1
        service()
    while done < len(tasks):
        tasks[done]()
        done += 1
    add_first()

    first_device = device == 0

    def finish(chunk):
        rows = rows_of(chunk)
        if chunk < 2:

            @pl.when(middle)
            def _():
                first_wait(3, chunk)

        else:
            first_wait(2, chunk)
            first_wait(3, chunk)
        has2 = device_bit(22).astype(F32)
        has3 = device_bit(23).astype(F32)
        part2 = rate[22, rows] * z_in[2, rows]
        if chunk < 2:
            part2 = jnp.where(middle, part2, z_in[2, rows])
        part3 = rate[23, rows] * z_in[3, rows]
        total = sum_f[rows] + part2 * has2 + part3 * has3
        if chunk == 0:
            spot = (iota((CHUNK, LANES), 0) == 0) & (iota((CHUNK, LANES), 1) == 0) & first_device
            total = total + jnp.where(spot, float(2**EVENTS), 0.0)
            values = total * inverse[rows]
            dist_ref[rows] = jnp.where(spot, 0.0, values)
        else:
            values = total * inverse[rows]
            dist_ref[rows] = values
        fwd[rows] = values
        pulled = sum_a[rows] + part2 * (1.0 - has2) + part3 * (1.0 - has3)
        weights = counts[rows] / (float(PATIENTS) * values)
        adj[rows] = (weights + pulled * 2.0**-12) * inverse[rows]

    for chunk in (2, 3, 0, 1):
        finish(chunk)
        if chunk < 2:
            send_adjoint(chunk)
        else:
            send_forward(chunk - 2)

    upper = pl.ds(HALF, HALF)
    lower = pl.ds(0, HALF)
    cross_start(fwd.at[upper], adj.at[lower], cross_half, h_send, h_recv)

    def put(column, total, parts):
        at = pl.ds(column * LANES, LANES)
        folded[0:8, at] = total
        for bit in range(6):
            folded[8 * bit + 8 : 8 * bit + 16, at] = parts[bit]

    def fold(values, bits):
        zero = jnp.zeros((8, LANES), F32)
        parts = [zero] * 6
        rest = values
        for position in reversed(range(len(bits))):
            size = 2**position
            high = rest[size:]
            parts[bits[position]] = jnp.sum(high, axis=0)
            rest = rest[:size] + high
        return rest[0], parts

    every = (0, 1, 2, 3, 4, 5)

    def gradient_lane(bit):
        def run():
            values = adj[...]
            moved = pltpu.roll(values, LANES - 2**bit, 1)
            term = rate[bit] * fwd[...] * (moved - values) * (1.0 - lane_has[bit])
            put(bit, *fold(term.reshape(64, 8, LANES), every))

        return run

    def gradient_sub(bit):
        def run():
            values = adj[...].reshape(64, 8, LANES)
            moved = pltpu.roll(values, 8 - 2**bit, 1)
            scaled = (rate[7 + bit] * fwd[...]).reshape(64, 8, LANES)
            term = scaled * (moved - values) * (1.0 - sub_has[bit])
            put(7 + bit, *fold(term, every))

        return run

    def gradient_row(bit):
        def run():
            distance = 8 * 2**bit
            shape = (ROWS // (2 * distance), 2, distance, LANES)
            values = adj[...].reshape(shape)
            rates = rate[10 + bit].reshape(shape)
            forwards = fwd[...].reshape(shape)
            term = rates[:, 0] * forwards[:, 0] * (values[:, 1] - values[:, 0])
            others = tuple(other for other in every if other != bit)
            put(10 + bit, *fold(term.reshape(32, 8, LANES), others))

        return run

    def gradient_pair(bit, from_above, from_below):
        has = device_bit(bit).astype(F32)
        lacks = 1.0 - has
        low = rate[bit, lower] * fwd[lower] * (from_above - adj[lower]) * lacks
        theirs = has * from_below - lacks * fwd[upper]
        high = rate[bit, upper] * adj[upper] * theirs
        term = jnp.concatenate([low, high], axis=0)
        put(bit, *fold(term.reshape(64, 8, LANES), every))

    def gradient_cross(number):
        def run():
            bit = CROSS[number][0]
            cross_copy(number, fwd.at[upper], cross_half, h_send, h_recv).wait_recv()
            gradient_pair(bit, cross_half[number], cross_half[number])

        return run

    def gradient_ring(bit):
        def run():
            if bit:
                for piece in range(PIECES):
                    z_wait(bit, piece)
            gradient_pair(20 + bit, half_in[bit], half_in[bit])

        return run

    def relay_all():
        for piece in range(PIECES):
            z_wait(0, piece)
            relay(piece)

    def likelihood():
        zero = [jnp.zeros((8, LANES), F32)] * 6
        logs = counts[...] * jnp.log(fwd[...])
        put(EVENTS, jnp.sum(logs.reshape(64, 8, LANES), axis=0), zero)
        spot = (iota((8, LANES), 0) == 0) & (iota((8, LANES), 1) == 0) & first_device
        put(EVENTS + 1, jnp.where(spot, jnp.log(fwd[0:8]), 0.0), zero)

    sub32 = iota((32, LANES), 0)
    lane32 = iota((32, LANES), 1)
    picker_sub = iota((32, 56), 0)
    picker_lane = iota((32, 56), 1)
    on_total = picker_lane < 8
    sub_part = (picker_lane >> jnp.clip(picker_sub - 7, 0, 2)) & 1
    is_sub = (picker_sub >= 7) & (picker_sub < 10)
    is_row = (picker_sub >= 10) & (picker_sub < 16)
    row_part = (picker_lane >> 3) == picker_sub - 9
    picker = jnp.where(
        is_sub,
        jnp.where(on_total, sub_part, 0),
        jnp.where(is_row, row_part.astype(jnp.int32), on_total.astype(jnp.int32)),
    ).astype(F32)
    lane_part = (lane32 >> jnp.minimum(sub32, 6)) & 1
    device_part = (device >> jnp.clip(sub32 - FIRST_DEVICE_BIT, 0, 8)) & 1
    weights32 = jnp.where(
        sub32 < 7,
        lane_part,
        jnp.where(sub32 < 16, 1, jnp.where(sub32 < EVENTS, device_part, (sub32 == EVENTS).astype(jnp.int32))),
    ).astype(F32)
    lane8 = iota((8, LANES), 1)

    def collect(columns):
        def run():
            tile = reduce_out[0]
            for column in columns:
                at = pl.ds(column * LANES, LANES)
                picked = nn(picker, folded[:, at]) * weights32
                sums = jnp.sum(jnp.where(sub32 == column, 0.0, picked) if column < EVENTS else picked, axis=1, keepdims=True)
                for group in range(4):
                    tile = jnp.where(
                        lane8 == 32 * group + column, sums[8 * group : 8 * group + 8], tile
                    )
            reduce_out[0] = tile

        return run

    reduce_out[0] = jnp.zeros((8, LANES), F32)
    tasks = [gradient_lane(bit) for bit in range(5)]
    tasks += [relay_all]
    tasks += [gradient_lane(bit) for bit in range(5, 7)]
    tasks += [gradient_sub(bit) for bit in range(3)]
    tasks += [gradient_row(bit) for bit in range(6)]
    tasks += [likelihood, gradient_ring(0)]
    tasks += [collect(tuple(range(16)) + (20, 25, 26))]
    tasks += [gradient_cross(number) for number in range(len(CROSS))]
    tasks += [collect((16, 17, 18, 19, 24))]
    for bit in (1, 2, 3):
        tasks += [gradient_ring(bit), collect((20 + bit,))]
    for task in tasks:
        task()

    for stage, peers in enumerate(STAGES):
        copies = []
        for number, (grp_distances, wide_distances) in enumerate(peers):
            where = {"grp": flip(grp, grp_distances), "wide": flip(wide, wide_distances)}
            copy = remote(
                reduce_out.at[stage],
                reduce_in.at[stage, number],
                r_send.at[stage, number],
                r_recv.at[stage, number],
                where,
            )
            begin(copy)
            copies.append(copy)
        for copy in copies:
            copy.wait_recv()
        parts = [reduce_out[stage]] + [reduce_in[stage, number] for number in range(len(peers))]
        while len(parts) > 1:
            parts = [low + high for low, high in zip(parts[0::2], parts[1::2])]
        reduce_out[stage + 1] = parts[0]

    tile = reduce_out[len(STAGES)]
    spread = jnp.concatenate(
        [tile] + [pltpu.roll(tile, LANES - 32 * group, 1) for group in range(1, 4)], axis=0
    )
    totals = spread[EVENTS : EVENTS + 1, :]
    inside = (sub32 < EVENTS) & (lane32 < EVENTS)
    matrix = jnp.where(inside, spread, 0.0)
    matrix = matrix + jnp.where(inside & (sub32 == lane32), totals, 0.0)
    matrix = jnp.concatenate([matrix, jnp.zeros((LANES - 32, LANES), F32)], axis=0)
    by_event = onehot[...]
    gradient = nt(nt(by_event[0:32], matrix), by_event)
    grad_ref[...] = gradient[0:EVENTS, 0:EVENTS]
    loglik_ref[0, 0] = jnp.sum(jnp.where((sub32 == EVENTS) & (lane32 == EVENTS), spread, 0.0)) / float(
        PATIENTS
    )
    empty_ref[0, 0] = jnp.sum(jnp.where((sub32 == EVENTS) & (lane32 == EVENTS + 1), spread, 0.0))

    for copy in started:
        copy.wait_send()
    for condition, copy in guarded:

        @pl.when(condition)
        def _():
            copy.wait_send()


def body(log_hazards, bit_order, patients, start_dist, start_adjoint):
    vmem = pl.BlockSpec(memory_space=pltpu.VMEM)
    smem = pl.BlockSpec(memory_space=pltpu.SMEM)
    dma = pltpu.SemaphoreType.DMA

    def block(*shape):
        return pltpu.VMEM(shape, F32)

    distribution, gradient, loglik, empty_state = pl.pallas_call(
        kernel,
        out_shape=(
            jax.ShapeDtypeStruct((ROWS, LANES), F32),
            jax.ShapeDtypeStruct((EVENTS, EVENTS), F32),
            jax.ShapeDtypeStruct((1, 1), F32),
            jax.ShapeDtypeStruct((1, 1), F32),
        ),
        in_specs=[pl.BlockSpec(memory_space=pl.ANY)] * 5,
        out_specs=(vmem, vmem, smem, smem),
        scratch_shapes=[
            block(EVENTS, EVENTS),
            pltpu.SMEM((EVENTS,), jnp.int32),
            pltpu.VMEM((PATIENTS // LANES, LANES), jnp.int32),
            block(ROWS, LANES),
            block(ROWS, LANES),
            block(EVENTS, ROWS, LANES),
            block(ROWS, LANES),
            block(ROWS, LANES),
            block(ROWS, LANES),
            block(ROWS, LANES),
            block(ROWS, LANES),
            block(ROWS, LANES),
            block(56, COLUMNS * LANES),
            block(4, ROWS, LANES),
            block(HALF, LANES),
            block(2, HALF, LANES),
            block(HALF, LANES),
            block(8, LANES),
            block(4, HALF, LANES),
            block(len(CROSS), ROWS, LANES),
            block(len(CROSS), HALF, LANES),
            block(len(STAGES) + 1, 8, LANES),
            block(len(STAGES), PEERS, 8, LANES),
            block(LANES, LANES),
            block(LANES, LANES),
            block(ROWS + 32, LANES),
            dma((8, CHUNKS)),
            dma((4, CHUNKS)),
            dma((2, CHUNKS)),
            dma((6, PIECES)),
            dma((4, PIECES)),
            dma((len(CROSS),)),
            dma((len(CROSS),)),
            dma((len(CROSS),)),
            dma((len(CROSS),)),
            dma((len(STAGES), PEERS)),
            dma((len(STAGES), PEERS)),
            dma((5,)),
        ],
        compiler_params=pltpu.CompilerParams(
            collective_id=0, has_side_effects=True, vmem_limit_bytes=60 * 2**20
        ),
    )(
        log_hazards,
        bit_order,
        patients.reshape(PATIENTS // LANES, LANES),
        start_dist.reshape(ROWS, LANES),
        start_adjoint.reshape(ROWS, LANES),
    )
    return distribution.reshape(-1), loglik.reshape(()), gradient, empty_state.reshape(())


def solution(mesh):
    return jax.shard_map(
        body,
        mesh=mesh,
        in_specs=(P(), P(), P(), P(("wide", "grp")), P(("wide", "grp"))),
        out_specs=(P(("wide", "grp")), P(), P(), P()),
        check_vma=False,
    )
```

```python
import jax
import jax.numpy as jnp
from jax import lax
from jax.experimental import pallas as pl
from jax.experimental.pallas import tpu as pltpu
from jax.sharding import PartitionSpec as P

MESH = pl.DeviceIdType.MESH
HIGH = lax.Precision.HIGHEST
F32 = jnp.float32

EVENTS = 25
PATIENTS = 256
LANES = 128
ROWS = 512
HALF = 256
CHUNK = 128
CHUNKS = 4
PIECES = 2
FIRST_DEVICE_BIT = 16
CROSS = ((16, "grp", 1), (17, "grp", 2), (18, "grp", 4), (19, "grp", 8), (24, "wide", 16))
STAGES = (
    (((1,), ()), ((2,), ()), ((1, 2), ()), ((), (16,)), ((1,), (16,)), ((2,), (16,)), ((1, 2), (16,))),
    (((4,), ()), ((8,), ()), ((4, 8), ())),
    tuple(((), tuple(2**bit for bit in range(4) if mask >> bit & 1)) for mask in range(1, 16)),
)
PEERS = max(len(peers) for peers in STAGES)
COLUMNS = EVENTS + 2
ORDER = (0, 2, 1, 3)


def nn(left, right):
    return lax.dot_general(
        left, right, (((1,), (0,)), ((), ())), precision=HIGH, preferred_element_type=F32
    )


def nt(left, right):
    return lax.dot_general(
        left, right, (((1,), (1,)), ((), ())), precision=HIGH, preferred_element_type=F32
    )


def iota(shape, axis):
    return lax.broadcasted_iota(jnp.int32, shape, axis)


def flip(index, distances):
    for distance in distances:
        index = index + distance - 2 * distance * ((index // distance) % 2)
    return index


def kernel(
    hazards_hbm,
    order_hbm,
    patients_hbm,
    p_hbm,
    q_hbm,
    dist_ref,
    grad_ref,
    loglik_ref,
    empty_ref,
    hazards_ref,
    order_ref,
    patients_ref,
    p_ref,
    q_ref,
    rate,
    inverse,
    sum_f,
    sum_a,
    fwd,
    adj,
    counts,
    folded,
    z_in,
    merge_in,
    wrap_in,
    merged,
    factor,
    half_in,
    cross_in,
    cross_half,
    reduce_out,
    reduce_in,
    onehot,
    hazards,
    tables,
    p_send,
    p_recv,
    m_recv,
    z_send,
    z_recv,
    x_send,
    x_recv,
    h_send,
    h_recv,
    r_send,
    r_recv,
    local_sem,
):
    wide = lax.axis_index("wide")
    grp = lax.axis_index("grp")
    device = wide * 16 + grp
    place = wide % 16

    def to_place(offset):
        return {"wide": wide - place + (place + offset + 16) % 16}

    def device_bit(bit):
        return (device // 2 ** (bit - FIRST_DEVICE_BIT)) % 2

    def partner(axis, distance):
        return {axis: flip(grp if axis == "grp" else wide, (distance,))}

    def remote(source, target, send, receive, where):
        return pltpu.make_async_remote_copy(
            src_ref=source,
            dst_ref=target,
            send_sem=send,
            recv_sem=receive,
            device_id=where,
            device_id_type=MESH,
        )

    local_copies = [
        pltpu.make_async_copy(source, target, local_sem.at[number])
        for number, (source, target) in enumerate(
            (
                (hazards_hbm, hazards_ref),
                (order_hbm, order_ref),
                (patients_hbm, patients_ref),
                (p_hbm, p_ref),
                (q_hbm, q_ref),
            )
        )
    ]
    for copy in local_copies:
        copy.start()

    barrier = pltpu.get_barrier_semaphore()
    neighbours = [to_place(offset) for offset in (-4, -3, -2, -1, 1, 2, 3, 4)]
    neighbours += [partner(axis, distance) for _, axis, distance in CROSS]
    for neighbour in neighbours:
        pl.semaphore_signal(barrier, inc=1, device_id=neighbour, device_id_type=MESH)
    pl.semaphore_wait(barrier, len(neighbours))

    started = []

    def rows_of(chunk):
        return pl.ds(chunk * CHUNK, CHUNK)

    odd = place % 2
    step_up = 2 * odd - 1

    def z_rows(piece):
        return pl.ds(piece * CHUNK, CHUNK)

    def z_copy(source, bit, piece, send, offset):
        return remote(
            source,
            half_in.at[bit, z_rows(piece)],
            z_send.at[send, piece],
            z_recv.at[bit, piece],
            {"wide": wide - place + (place + offset + 16) % 16},
        )

    guarded = []

    def begin_if(condition, copy):
        @pl.when(condition)
        def _():
            copy.start()

        guarded.append((condition, copy))

    def forward_piece(piece):
        return fwd.at[pl.ds(HALF + piece * CHUNK, CHUNK)]

    def adjoint_piece(piece):
        return adj.at[z_rows(piece)]

    def differs(bit):
        return (place // 2**bit) % 2 != odd

    def send_forward(piece):
        source = forward_piece(piece)
        begin_if(odd == 0, z_copy(source, 0, piece, 0, 1))
        begin_if((place // 8) % 2 == 0, z_copy(source, 3, piece, 1, 8))
        for bit in (2, 1):
            begin_if(differs(bit) & (odd == 1), z_copy(source, bit, piece, 1 + bit, 2**bit))

    def send_adjoint(piece):
        source = adjoint_piece(piece)
        begin_if(odd == 1, z_copy(source, 0, piece, 0, -1))
        begin_if((place // 8) % 2 == 1, z_copy(source, 3, piece, 1, -8))
        for bit in (2, 1):
            begin_if(differs(bit) & (odd == 0), z_copy(source, bit, piece, 1 + bit, -(2**bit)))

    def relay(piece):
        source = half_in.at[0, z_rows(piece)]
        for bit in (2, 1):
            begin_if(
                differs(bit), z_copy(source, bit, piece, 3 + bit, step_up * (2**bit - 1))
            )

    def z_wait(bit, piece):
        z_copy(adjoint_piece(piece), bit, piece, 0, 1).wait_recv()

    def begin(copy):
        copy.start()
        started.append(copy)

    top = (place // 8) % 2
    middle = top != (place // 4) % 2
    end = top == (place // 4) % 2
    toward = 4 - 8 * top

    def first_copy(source, bit, chunk, send, offset):
        rows = rows_of(chunk)
        return remote(
            source, z_in.at[bit, rows], p_send.at[send, chunk], p_recv.at[bit, chunk], to_place(offset)
        )

    def first_wait(bit, chunk):
        first_copy(p_hbm.at[rows_of(chunk)], bit, chunk, 0, 1).wait_recv()

    def half_rows(chunk):
        return pl.ds((chunk % 2) * CHUNK, CHUNK)

    def first_leg(source, chunk, side):
        if chunk < 2:
            target, semaphore, offset = merge_in.at[half_rows(chunk)], m_recv.at[0, chunk], toward
        else:
            target, semaphore, offset = wrap_in.at[side, half_rows(chunk)], m_recv.at[side, chunk], -toward
        return remote(source, target, p_send.at[5, chunk], semaphore, to_place(offset))

    def start_far(chunk):
        rows = rows_of(chunk)
        for value, source in ((0, p_hbm.at[rows]), (1, q_hbm.at[rows])):
            ready = (top == value) & middle if chunk < 2 else top == value
            begin_if(ready, first_leg(source, chunk, value))

    def start_neighbour(chunk):
        rows = rows_of(chunk)
        begin_if(odd == 0, first_copy(p_hbm.at[rows], 0, chunk, 0, 1))
        begin_if(odd == 1, first_copy(q_hbm.at[rows], 0, chunk, 0, -1))

    def start_own(chunk):
        rows = rows_of(chunk)
        for bit in (2, 1):
            wanted = differs(bit) & end if bit == 2 and chunk < 2 else differs(bit)
            begin_if(wanted & (odd == 1), first_copy(p_hbm.at[rows], bit, chunk, bit, 2**bit))
            begin_if(wanted & (odd == 0), first_copy(q_hbm.at[rows], bit, chunk, bit, -(2**bit)))

    for chunk in ORDER:
        start_far(chunk)
    for chunk in ORDER:
        start_neighbour(chunk)
    for chunk in ORDER:
        start_own(chunk)

    def pass_neighbour(chunk):
        def run():
            first_wait(0, chunk)
            source = z_in.at[0, rows_of(chunk)]
            for bit in (2, 1):
                wanted = differs(bit) & end if bit == 2 and chunk < 2 else differs(bit)
                begin_if(wanted, first_copy(source, bit, chunk, 2 + bit, step_up * (2**bit - 1)))

        return run

    def pass_wrap(chunk):
        def run():
            rows = half_rows(chunk)
            for side, offset in ((0, -4), (1, 4)):
                source = wrap_in.at[side, rows]

                @pl.when(end)
                def _():
                    remote(
                        source, source, p_send.at[5, chunk], m_recv.at[side, chunk], to_place(4)
                    ).wait_recv()

                begin_if(end, first_copy(source, 3, chunk, 6 + side, offset))

        return run

    def pass_merged(chunk):
        def run():
            rows = rows_of(chunk)
            source = merge_in.at[rows]

            @pl.when(middle)
            def _():
                remote(source, source, p_send.at[5, chunk], m_recv.at[0, chunk], to_place(4)).wait_recv()
                high = top.astype(F32)
                own = high * p_ref[rows] + (1.0 - high) * q_ref[rows]
                far = rate[23, rows] * factor[0:1, :] * merge_in[rows]
                merged[rows] = far + rate[22, rows] * own

            begin_if(middle, first_copy(merged.at[rows], 2, chunk, 7, -toward))

        return run

    def pass_second(chunk):
        def run():
            first_wait(2, chunk)
            begin_if(middle, first_copy(z_in.at[2, rows_of(chunk)], 3, chunk, 6, toward))

        return run

    def cross_copy(number, source, target, send, receive):
        _, axis, distance = CROSS[number]
        return remote(
            source, target.at[number], send.at[number], receive.at[number], partner(axis, distance)
        )

    def cross_start(low, high, target, send, receive):
        for number, (bit, _, _) in enumerate(CROSS):
            for value, source in ((0, low), (1, high)):

                @pl.when(device_bit(bit) == value)
                def _():
                    cross_copy(number, source, target, send, receive).start()

            started.append(cross_copy(number, low, target, send, receive))

    cross_start(p_hbm, q_hbm, cross_in, x_send, x_recv)

    lane_id = iota((1, LANES), 1)
    lane_has = [((lane_id >> bit) & 1).astype(F32) for bit in range(7)]
    sub_id = iota((1, 8, LANES), 1)
    sub_has = [((sub_id >> bit) & 1).astype(F32) for bit in range(3)]

    def make_tables():
        lane8 = iota((8, LANES), 1)
        sub8 = iota((8, LANES), 0)
        hazards[...] = jnp.zeros_like(hazards)
        hazards[0:EVENTS, 0:EVENTS] = hazards_ref[...]
        onehot[...] = jnp.zeros_like(onehot)
        for tile in range(4):
            block = jnp.zeros((8, LANES), F32)
            for event in range(8 * tile, min(8 * tile + 8, EVENTS)):
                hit = (sub8 == event - 8 * tile) & (lane8 == order_ref[event])
                block = jnp.where(hit, 1.0, block)
            onehot[8 * tile : 8 * tile + 8, :] = block
        by_event = onehot[...]
        by_bit = by_event.T
        matrix = nn(by_bit, nn(hazards[...], by_event))
        square = (LANES, LANES)
        sub = iota(square, 0)
        lane = iota(square, 1)
        same = sub == lane
        diagonal = jnp.sum(jnp.where(same, matrix, 0.0), axis=1, keepdims=True)
        coupling = jnp.where(same, 0.0, matrix)
        sign = (2 * top - 1).astype(F32)
        factor[...] = jnp.broadcast_to(jnp.exp(coupling[23:24, 22:23] * sign), (8, LANES))
        lane_bits = jnp.where(sub < 7, (lane >> jnp.minimum(sub, 7)) & 1, 0).astype(F32)
        tables[ROWS : ROWS + 32, :] = jnp.exp(nn(coupling[0:32], lane_bits))
        row = iota((ROWS, LANES), 0)
        column = iota((ROWS, LANES), 1)
        row_bit = (row >> jnp.clip(column - 7, 0, 8)) & 1
        dev_bit = (device >> jnp.clip(column - FIRST_DEVICE_BIT, 0, 8)) & 1
        bits = jnp.where(column < 7, 0, jnp.where(column < 16, row_bit, dev_bit))
        features = jnp.where(column < EVENTS, bits, jnp.where(column == EVENTS, 1, 0)).astype(F32)
        widened = jnp.where(lane == EVENTS, diagonal, coupling)
        tables[0:ROWS, :] = jnp.exp(nt(features, widened))

    def make_rate(bit):
        def run():
            row_factor = tables[0:ROWS, bit : bit + 1]
            lane_factor = tables[ROWS + bit : ROWS + bit + 1, :]
            rate[bit] = row_factor * lane_factor

        return run

    def chunk_groups(values):
        return values.reshape(CHUNK // 8, 8, LANES)

    def lower_rows(values, distance):
        split = values.reshape(CHUNK // (2 * distance), 2, distance, LANES)
        low = split[:, 0:1]
        return jnp.concatenate([low, jnp.zeros_like(low)], axis=1).reshape(CHUNK, LANES)

    def make_inverse(chunk):
        def run():
            rows = rows_of(chunk)
            total = jnp.ones((CHUNK, LANES), F32)
            for bit in range(7):
                total = total + rate[bit, rows] * (1.0 - lane_has[bit])
            for bit in range(3):
                part = chunk_groups(rate[7 + bit, rows]) * (1.0 - sub_has[bit])
                total = total + part.reshape(CHUNK, LANES)
            for bit in range(4):
                total = total + lower_rows(rate[10 + bit, rows], 8 * 2**bit)
            if chunk % 2 == 0:
                total = total + rate[14, rows]
            if chunk < 2:
                total = total + rate[15, rows]
            for bit in range(FIRST_DEVICE_BIT, EVENTS):
                total = total + rate[bit, rows] * (1 - device_bit(bit)).astype(F32)
            inverse[rows] = 1.0 / total

        return run

    def local_forward(chunk):
        def run():
            rows = rows_of(chunk)
            values = p_ref[rows]
            total = jnp.zeros((CHUNK, LANES), F32)
            for bit in range(7):
                total = total + pltpu.roll(rate[bit, rows] * values, 2**bit, 1) * lane_has[bit]
            for bit in range(3):
                moved = pltpu.roll(chunk_groups(rate[7 + bit, rows] * values), 2**bit, 1)
                total = total + (moved * sub_has[bit]).reshape(CHUNK, LANES)
            for bit in range(4):
                distance = 8 * 2**bit
                split = (rate[10 + bit, rows] * values).reshape(
                    CHUNK // (2 * distance), 2, distance, LANES
                )
                low = split[:, 0:1]
                total = total + jnp.concatenate([jnp.zeros_like(low), low], axis=1).reshape(
                    CHUNK, LANES
                )
            if chunk % 2 == 1:
                other = rows_of(chunk - 1)
                total = total + rate[14, other] * p_ref[other]
            if chunk >= 2:
                other = rows_of(chunk - 2)
                total = total + rate[15, other] * p_ref[other]
            sum_f[rows] = total

        return run

    def local_adjoint(chunk):
        def run():
            rows = rows_of(chunk)
            values = q_ref[rows]
            total = jnp.zeros((CHUNK, LANES), F32)
            for bit in range(7):
                moved = pltpu.roll(values, LANES - 2**bit, 1)
                total = total + rate[bit, rows] * moved * (1.0 - lane_has[bit])
            grouped = chunk_groups(values)
            for bit in range(3):
                moved = pltpu.roll(grouped, 8 - 2**bit, 1) * (1.0 - sub_has[bit])
                total = total + rate[7 + bit, rows] * moved.reshape(CHUNK, LANES)
            for bit in range(4):
                distance = 8 * 2**bit
                split = values.reshape(CHUNK // (2 * distance), 2, distance, LANES)
                rates = rate[10 + bit, rows].reshape(split.shape)
                low = rates[:, 0:1] * split[:, 1:2]
                total = total + jnp.concatenate([low, jnp.zeros_like(low)], axis=1).reshape(
                    CHUNK, LANES
                )
            if chunk % 2 == 0:
                total = total + rate[14, rows] * q_ref[rows_of(chunk + 1)]
            if chunk < 2:
                total = total + rate[15, rows] * q_ref[rows_of(chunk + 2)]
            sum_a[rows] = total

        return run

    def make_counts():
        total = jnp.zeros((ROWS, LANES), F32)
        for part in range(PATIENTS // LANES):
            people = patients_ref[part : part + 1, :]
            state = jnp.zeros((1, LANES), jnp.int32)
            for event in range(EVENTS):
                state = state + (((people >> event) & 1) << order_ref[event])
            here = (state >> 16) == device
            row = jnp.where(here, (state >> 7) & (ROWS - 1), -1)
            lane = state & (LANES - 1)
            in_row = jnp.where(iota((ROWS, LANES), 0) == row, 1.0, 0.0)
            in_lane = jnp.where(iota((LANES, LANES), 0) == lane, 1.0, 0.0)
            total = total + lax.dot_general(
                in_row.astype(jnp.bfloat16),
                in_lane.astype(jnp.bfloat16),
                (((1,), (1,)), ((), ())),
                preferred_element_type=F32,
            )
        counts[...] = total

    def add_pair(bit, received):
        has = device_bit(bit).astype(F32)
        term = rate[bit] * received[...]
        sum_f[...] += term * has
        sum_a[...] += term * (1.0 - has)

    def add_cross(number):
        def run():
            bit = CROSS[number][0]
            cross_copy(number, p_hbm, cross_in, x_send, x_recv).wait_recv()
            add_pair(bit, cross_in.at[number])

        return run

    def land():
        for copy in local_copies:
            copy.wait()

    def add_first():
        for chunk in ORDER:
            first_wait(1, chunk)
        add_pair(20, z_in.at[0])
        add_pair(21, z_in.at[1])

    @pl.when(end)
    def _():
        z_in[3, 0:HALF] = jnp.zeros((HALF, LANES), F32)

    tasks = [land, make_tables, make_rate(22), make_rate(23)]
    tasks += [make_rate(bit) for bit in range(EVENTS) if bit not in (22, 23)]
    tasks += [make_counts]
    for chunk in range(CHUNKS):
        tasks += [make_inverse(chunk), local_forward(chunk), local_adjoint(chunk)]
    tasks += [add_cross(number) for number in range(len(CROSS))]
    services = [
        pass_wrap(2),
        pass_merged(0),
        pass_wrap(3),
        pass_merged(1),
        pass_neighbour(0),
        pass_neighbour(2),
        pass_neighbour(1),
        pass_neighbour(3),
        pass_second(0),
        pass_second(1),
    ]
    done = 0
    for number, service in enumerate(services):
        goal = 6 + 2 * number
        while done < goal:
            tasks[done]()
            done += 1
        service()
    while done < len(tasks):
        tasks[done]()
        done += 1
    add_first()

    first_device = device == 0

    def finish(chunk):
        rows = rows_of(chunk)
        if chunk < 2:

            @pl.when(middle)
            def _():
                first_wait(3, chunk)

        else:
            first_wait(2, chunk)
            first_wait(3, chunk)
        has2 = device_bit(22).astype(F32)
        has3 = device_bit(23).astype(F32)
        part2 = rate[22, rows] * z_in[2, rows]
        if chunk < 2:
            part2 = jnp.where(middle, part2, z_in[2, rows])
        part3 = rate[23, rows] * z_in[3, rows]
        total = sum_f[rows] + part2 * has2 + part3 * has3
        if chunk == 0:
            spot = (iota((CHUNK, LANES), 0) == 0) & (iota((CHUNK, LANES), 1) == 0) & first_device
            total = total + jnp.where(spot, float(2**EVENTS), 0.0)
            values = total * inverse[rows]
            dist_ref[rows] = jnp.where(spot, 0.0, values)
        else:
            values = total * inverse[rows]
            dist_ref[rows] = values
        fwd[rows] = values
        pulled = sum_a[rows] + part2 * (1.0 - has2) + part3 * (1.0 - has3)
        weights = counts[rows] / (float(PATIENTS) * values)
        adj[rows] = (weights + pulled * 2.0**-12) * inverse[rows]

    for chunk in (2, 3, 0, 1):
        finish(chunk)
        if chunk < 2:
            send_adjoint(chunk)
        else:
            send_forward(chunk - 2)

    upper = pl.ds(HALF, HALF)
    lower = pl.ds(0, HALF)
    cross_start(fwd.at[upper], adj.at[lower], cross_half, h_send, h_recv)

    def put(column, total, parts):
        at = pl.ds(column * LANES, LANES)
        folded[0:8, at] = total
        for bit in range(6):
            folded[8 * bit + 8 : 8 * bit + 16, at] = parts[bit]

    def fold(values, bits):
        zero = jnp.zeros((8, LANES), F32)
        parts = [zero] * 6
        rest = values
        for position in reversed(range(len(bits))):
            size = 2**position
            high = rest[size:]
            parts[bits[position]] = jnp.sum(high, axis=0)
            rest = rest[:size] + high
        return rest[0], parts

    every = (0, 1, 2, 3, 4, 5)

    def gradient_lane(bit):
        def run():
            values = adj[...]
            moved = pltpu.roll(values, LANES - 2**bit, 1)
            term = rate[bit] * fwd[...] * (moved - values) * (1.0 - lane_has[bit])
            put(bit, *fold(term.reshape(64, 8, LANES), every))

        return run

    def gradient_sub(bit):
        def run():
            values = adj[...].reshape(64, 8, LANES)
            moved = pltpu.roll(values, 8 - 2**bit, 1)
            scaled = (rate[7 + bit] * fwd[...]).reshape(64, 8, LANES)
            term = scaled * (moved - values) * (1.0 - sub_has[bit])
            put(7 + bit, *fold(term, every))

        return run

    def gradient_row(bit):
        def run():
            distance = 8 * 2**bit
            shape = (ROWS // (2 * distance), 2, distance, LANES)
            values = adj[...].reshape(shape)
            rates = rate[10 + bit].reshape(shape)
            forwards = fwd[...].reshape(shape)
            term = rates[:, 0] * forwards[:, 0] * (values[:, 1] - values[:, 0])
            others = tuple(other for other in every if other != bit)
            put(10 + bit, *fold(term.reshape(32, 8, LANES), others))

        return run

    def gradient_pair(bit, from_above, from_below):
        has = device_bit(bit).astype(F32)
        lacks = 1.0 - has
        low = rate[bit, lower] * fwd[lower] * (from_above - adj[lower]) * lacks
        theirs = has * from_below - lacks * fwd[upper]
        high = rate[bit, upper] * adj[upper] * theirs
        term = jnp.concatenate([low, high], axis=0)
        put(bit, *fold(term.reshape(64, 8, LANES), every))

    def gradient_cross(number):
        def run():
            bit = CROSS[number][0]
            cross_copy(number, fwd.at[upper], cross_half, h_send, h_recv).wait_recv()
            gradient_pair(bit, cross_half[number], cross_half[number])

        return run

    def gradient_ring(bit):
        def run():
            if bit:
                for piece in range(PIECES):
                    z_wait(bit, piece)
            gradient_pair(20 + bit, half_in[bit], half_in[bit])

        return run

    def relay_all():
        for piece in range(PIECES):
            z_wait(0, piece)
            relay(piece)

    def likelihood():
        zero = [jnp.zeros((8, LANES), F32)] * 6
        logs = counts[...] * jnp.log(fwd[...])
        put(EVENTS, jnp.sum(logs.reshape(64, 8, LANES), axis=0), zero)
        spot = (iota((8, LANES), 0) == 0) & (iota((8, LANES), 1) == 0) & first_device
        put(EVENTS + 1, jnp.where(spot, jnp.log(fwd[0:8]), 0.0), zero)

    sub32 = iota((32, LANES), 0)
    lane32 = iota((32, LANES), 1)
    picker_sub = iota((32, 56), 0)
    picker_lane = iota((32, 56), 1)
    on_total = picker_lane < 8
    sub_part = (picker_lane >> jnp.clip(picker_sub - 7, 0, 2)) & 1
    is_sub = (picker_sub >= 7) & (picker_sub < 10)
    is_row = (picker_sub >= 10) & (picker_sub < 16)
    row_part = (picker_lane >> 3) == picker_sub - 9
    picker = jnp.where(
        is_sub,
        jnp.where(on_total, sub_part, 0),
        jnp.where(is_row, row_part.astype(jnp.int32), on_total.astype(jnp.int32)),
    ).astype(F32)
    lane_part = (lane32 >> jnp.minimum(sub32, 6)) & 1
    device_part = (device >> jnp.clip(sub32 - FIRST_DEVICE_BIT, 0, 8)) & 1
    weights32 = jnp.where(
        sub32 < 7,
        lane_part,
        jnp.where(sub32 < 16, 1, jnp.where(sub32 < EVENTS, device_part, (sub32 == EVENTS).astype(jnp.int32))),
    ).astype(F32)
    lane8 = iota((8, LANES), 1)

    def collect(columns):
        def run():
            tile = reduce_out[0]
            for column in columns:
                at = pl.ds(column * LANES, LANES)
                picked = nn(picker, folded[:, at]) * weights32
                sums = jnp.sum(jnp.where(sub32 == column, 0.0, picked) if column < EVENTS else picked, axis=1, keepdims=True)
                for group in range(4):
                    tile = jnp.where(
                        lane8 == 32 * group + column, sums[8 * group : 8 * group + 8], tile
                    )
            reduce_out[0] = tile

        return run

    reduce_out[0] = jnp.zeros((8, LANES), F32)
    tasks = [gradient_lane(bit) for bit in range(5)]
    tasks += [relay_all]
    tasks += [gradient_lane(bit) for bit in range(5, 7)]
    tasks += [gradient_sub(bit) for bit in range(3)]
    tasks += [gradient_row(bit) for bit in range(6)]
    tasks += [likelihood, gradient_ring(0)]
    tasks += [collect(tuple(range(16)) + (20, 25, 26))]
    tasks += [gradient_cross(number) for number in range(len(CROSS))]
    tasks += [collect((16, 17, 18, 19, 24))]
    tasks += [gradient_ring(1), gradient_ring(2), collect((21, 22)), gradient_ring(3), collect((23,))]
    for task in tasks:
        task()

    for stage, peers in enumerate(STAGES):
        copies = []
        for number, (grp_distances, wide_distances) in enumerate(peers):
            where = {"grp": flip(grp, grp_distances), "wide": flip(wide, wide_distances)}
            copy = remote(
                reduce_out.at[stage],
                reduce_in.at[stage, number],
                r_send.at[stage, number],
                r_recv.at[stage, number],
                where,
            )
            begin(copy)
            copies.append(copy)
        for copy in copies:
            copy.wait_recv()
        parts = [reduce_out[stage]] + [reduce_in[stage, number] for number in range(len(peers))]
        while len(parts) > 1:
            parts = [low + high for low, high in zip(parts[0::2], parts[1::2])]
        reduce_out[stage + 1] = parts[0]

    tile = reduce_out[len(STAGES)]
    spread = jnp.concatenate(
        [tile] + [pltpu.roll(tile, LANES - 32 * group, 1) for group in range(1, 4)], axis=0
    )
    totals = spread[EVENTS : EVENTS + 1, :]
    inside = (sub32 < EVENTS) & (lane32 < EVENTS)
    matrix = jnp.where(inside, spread, 0.0)
    matrix = matrix + jnp.where(inside & (sub32 == lane32), totals, 0.0)
    matrix = jnp.concatenate([matrix, jnp.zeros((LANES - 32, LANES), F32)], axis=0)
    by_event = onehot[...]
    gradient = nt(nt(by_event[0:32], matrix), by_event)
    grad_ref[...] = gradient[0:EVENTS, 0:EVENTS]
    loglik_ref[0, 0] = jnp.sum(jnp.where((sub32 == EVENTS) & (lane32 == EVENTS), spread, 0.0)) / float(
        PATIENTS
    )
    empty_ref[0, 0] = jnp.sum(jnp.where((sub32 == EVENTS) & (lane32 == EVENTS + 1), spread, 0.0))

    for copy in started:
        copy.wait_send()
    for condition, copy in guarded:

        @pl.when(condition)
        def _():
            copy.wait_send()


def body(log_hazards, bit_order, patients, start_dist, start_adjoint):
    vmem = pl.BlockSpec(memory_space=pltpu.VMEM)
    smem = pl.BlockSpec(memory_space=pltpu.SMEM)
    dma = pltpu.SemaphoreType.DMA

    def block(*shape):
        return pltpu.VMEM(shape, F32)

    distribution, gradient, loglik, empty_state = pl.pallas_call(
        kernel,
        out_shape=(
            jax.ShapeDtypeStruct((ROWS, LANES), F32),
            jax.ShapeDtypeStruct((EVENTS, EVENTS), F32),
            jax.ShapeDtypeStruct((1, 1), F32),
            jax.ShapeDtypeStruct((1, 1), F32),
        ),
        in_specs=[pl.BlockSpec(memory_space=pl.ANY)] * 5,
        out_specs=(vmem, vmem, smem, smem),
        scratch_shapes=[
            block(EVENTS, EVENTS),
            pltpu.SMEM((EVENTS,), jnp.int32),
            pltpu.VMEM((PATIENTS // LANES, LANES), jnp.int32),
            block(ROWS, LANES),
            block(ROWS, LANES),
            block(EVENTS, ROWS, LANES),
            block(ROWS, LANES),
            block(ROWS, LANES),
            block(ROWS, LANES),
            block(ROWS, LANES),
            block(ROWS, LANES),
            block(ROWS, LANES),
            block(56, COLUMNS * LANES),
            block(4, ROWS, LANES),
            block(HALF, LANES),
            block(2, HALF, LANES),
            block(HALF, LANES),
            block(8, LANES),
            block(4, HALF, LANES),
            block(len(CROSS), ROWS, LANES),
            block(len(CROSS), HALF, LANES),
            block(len(STAGES) + 1, 8, LANES),
            block(len(STAGES), PEERS, 8, LANES),
            block(LANES, LANES),
            block(LANES, LANES),
            block(ROWS + 32, LANES),
            dma((8, CHUNKS)),
            dma((4, CHUNKS)),
            dma((2, CHUNKS)),
            dma((6, PIECES)),
            dma((4, PIECES)),
            dma((len(CROSS),)),
            dma((len(CROSS),)),
            dma((len(CROSS),)),
            dma((len(CROSS),)),
            dma((len(STAGES), PEERS)),
            dma((len(STAGES), PEERS)),
            dma((5,)),
        ],
        compiler_params=pltpu.CompilerParams(
            collective_id=0, has_side_effects=True, vmem_limit_bytes=60 * 2**20
        ),
    )(
        log_hazards,
        bit_order,
        patients.reshape(PATIENTS // LANES, LANES),
        start_dist.reshape(ROWS, LANES),
        start_adjoint.reshape(ROWS, LANES),
    )
    return distribution.reshape(-1), loglik.reshape(()), gradient, empty_state.reshape(())


def solution(mesh):
    return jax.shard_map(
        body,
        mesh=mesh,
        in_specs=(P(), P(), P(), P(("wide", "grp")), P(("wide", "grp"))),
        out_specs=(P(("wide", "grp")), P(), P(), P()),
        check_vma=False,
    )
```
